512 devices in a mesh: row: 16 (over z, y_lo), col: 32 (over x, y_hi, core).
Axes of the slice: x: 4, y: 8 (y_hi: 4, y_lo: 2; y = y_hi * 2 + y_lo), z: 8, core: 2. Of those that a mesh axis runs over, the one named last changes fastest.
Arguments:
- features: bfloat16 [65536, 128], P(('col', 'row')), may hold values from -6 to 6
- grad_out: bfloat16 [65536, 128], P(('row', 'col')), may hold values from -6 to 6
- weight: bfloat16 [128, 128], replicated, may hold values from -0.5 to 0.5
- block_ids: int32 [16, 32, 152], P('row', 'col'), may hold values from 0 to 511, as said below
- block_vals: bfloat16 [16, 32, 152, 128, 128], P('row', 'col'), may hold values from -0.0390625 to 0.0390625
- block_count: int32 [16, 32], P('row', 'col'), may hold values from 1 to 152
- node_perm: int32 [512, 128], P(('col', 'row')), may hold values from 0 to 127, each once within a row
Outputs:
- feature_grad: bfloat16 [65536, 128], P(('col', 'row'))
- weight_grad: float32 [128, 128], replicated
The draws below stay inside these ranges and needn't reach their ends.
Inputs may be any that keep to these rules, and one draw needn't show every extreme that they name: `block_ids`: in each tile the 152 entries are distinct block positions p * 16 + q; slots at or beyond block_count are empty and must be ignored. `node_perm`: each row is a permutation of 0 to 127.
All inputs are finite; a program needn't handle non-finite values.
Results may differ from the reference program's by a relative error of at most 0.0059.
Values may be sent and summed in bfloat16 or wider, within the bound.
A program may use at most 128 MiB of HBM per device.

```python
import math
import jax
import jax.numpy as jnp
from jax import lax

HIDDEN_SIZE = 128
BLOCK = 128
NODES_DEV = 128
GRID_ROWS = 16
GRID_COLS = 32
NODES = 65536
ROW_BLOCKS = 32
COL_BLOCKS = 16
SLOTS = 512
BLOCKS_TILE = 152


def draw_block_ids(key, part):
    keys = jax.random.split(key, GRID_ROWS * GRID_COLS)

    def one_tile(tile_key):
        chosen = jax.random.permutation(tile_key, SLOTS)[:BLOCKS_TILE].astype(jnp.int32)
        present = jnp.any(chosen == SLOTS - 1)
        return jnp.where(present, chosen, chosen.at[0].set(SLOTS - 1))
    return jax.vmap(one_tile)(keys).reshape(GRID_ROWS, GRID_COLS, BLOCKS_TILE).astype(jnp.int32)


def draw_block_count(key, part):
    uniform_ints = jax.random.randint(key, (GRID_ROWS * GRID_COLS,), 0, BLOCKS_TILE)
    counts = 1 + uniform_ints * uniform_ints // BLOCKS_TILE
    chosen_tile = jax.random.randint(jax.random.fold_in(key, 7), (), 0, GRID_ROWS * GRID_COLS)
    counts = jnp.where(jnp.arange(GRID_ROWS * GRID_COLS) == chosen_tile, BLOCKS_TILE, counts)
    return counts.reshape(GRID_ROWS, GRID_COLS).astype(jnp.int32)


def level_of(rng, extent, pieces, least, top_value):
    loudness = 1.0
    for position, shards_of in pieces:
        draws = jax.random.uniform(jax.random.fold_in(jax.random.fold_in(rng, 6), position), (shards_of,), jnp.float32, least / len(pieces), top_value / len(pieces))
        loudness = loudness * jnp.repeat(jnp.exp(draws), extent[position] // shards_of).reshape((-1,) + (1,) * (len(extent) - 1 - position))
    return loudness


def gaussian(key, extent, deviation, bound, shards=(), kind=jnp.bfloat16):
    level = level_of(key, extent, shards, -0.22, 0.18) if shards else 1.0
    drawn = jax.random.normal(key, extent, jnp.float32) * deviation * level
    return jnp.minimum(jnp.maximum(drawn, -bound), bound).astype(kind)


def setup_inputs(seed: int = 0) -> dict:
    key_of = jax.random.split(jax.random.key(seed), 8)
    features = gaussian(key_of[0], (NODES, HIDDEN_SIZE), 1.0, 6.0, ((0, 512),))
    grad_out = gaussian(key_of[1], (NODES, HIDDEN_SIZE), 1.0, 6.0, ((0, 512),))
    weight = gaussian(key_of[2], (HIDDEN_SIZE, HIDDEN_SIZE), HIDDEN_SIZE ** -0.5, 0.5)
    block_ids = draw_block_ids(jax.random.fold_in(key_of[7], 71), 0)
    block_vals = gaussian(key_of[4], (GRID_ROWS, GRID_COLS, BLOCKS_TILE, BLOCK, BLOCK), (BLOCKS_TILE * BLOCK * BLOCK // NODES_DEV) ** -0.5, 0.0390625, ((0, 16), (1, 32)))
    block_count = draw_block_count(jax.random.fold_in(key_of[7], 71), 0)
    node_perm = jax.vmap(lambda own: jax.random.permutation(own, NODES_DEV))(jax.random.split(key_of[6], (GRID_ROWS * GRID_COLS))).reshape((GRID_ROWS * GRID_COLS, NODES_DEV)).astype(jnp.int32)
    return {"features": features, "grad_out": grad_out, "weight": weight, "block_ids": block_ids, "block_vals": block_vals, "block_count": block_count, "node_perm": node_perm}


def reference(features, grad_out, weight, block_ids, block_vals, block_count, node_perm):
    tile_rows = ROW_BLOCKS * BLOCK
    tile_cols = COL_BLOCKS * BLOCK
    slot_index = jnp.arange(BLOCKS_TILE, dtype=jnp.int32)
    grid_total = GRID_ROWS * GRID_COLS

    def forward_tile(tile, total):
        tile = jnp.asarray(tile).astype(jnp.int32)
        grid_r = tile // GRID_COLS
        grid_c = tile % GRID_COLS
        tile_ids = block_ids[grid_r, grid_c]
        values = block_vals[grid_r, grid_c].astype(jnp.float32)
        live = (slot_index < block_count[grid_r, grid_c]).astype(jnp.float32)
        source = lax.dynamic_slice_in_dim(features, (grid_c * tile_cols).astype(jnp.int32), tile_cols, 0)
        source = source.astype(jnp.float32).reshape(COL_BLOCKS, BLOCK, HIDDEN_SIZE)
        picked = source[tile_ids % COL_BLOCKS]
        product = jnp.einsum('kij,kjf->kif', values, picked, precision=lax.Precision.HIGHEST)
        product = product * live[:, None, None]
        partial_value = jax.ops.segment_sum(product, tile_ids // COL_BLOCKS, num_segments=ROW_BLOCKS)
        partial_value = partial_value.reshape(tile_rows, HIDDEN_SIZE)
        start = (grid_r * tile_rows).astype(jnp.int32)
        current = lax.dynamic_slice_in_dim(total, start, tile_rows, 0)
        return lax.dynamic_update_slice_in_dim(total, current + partial_value, start, 0)
    aggregate = lax.fori_loop(0, grid_total, forward_tile, jnp.zeros((NODES, HIDDEN_SIZE), jnp.float32))
    agg_low = aggregate.astype(jnp.bfloat16)
    pre = jnp.dot(agg_low, weight, preferred_element_type=jnp.float32)
    sigma = jax.nn.sigmoid(pre)
    grad_pre = (grad_out.astype(jnp.float32) * sigma * (1.0 + pre * (1.0 - sigma))).astype(jnp.bfloat16)
    weight_grad = jnp.dot(agg_low.T, grad_pre, preferred_element_type=jnp.float32) * (1.0 / math.sqrt(NODES))
    grad_agg = jnp.dot(grad_pre, weight.T, preferred_element_type=jnp.float32).astype(jnp.bfloat16)

    def backward_tile(tile, total):
        tile = jnp.asarray(tile).astype(jnp.int32)
        grid_r = tile // GRID_COLS
        grid_c = tile % GRID_COLS
        tile_ids = block_ids[grid_r, grid_c]
        values = block_vals[grid_r, grid_c].astype(jnp.float32)
        live = (slot_index < block_count[grid_r, grid_c]).astype(jnp.float32)
        source = lax.dynamic_slice_in_dim(grad_agg, (grid_r * tile_rows).astype(jnp.int32), tile_rows, 0)
        source = source.astype(jnp.float32).reshape(ROW_BLOCKS, BLOCK, HIDDEN_SIZE)
        picked = source[tile_ids // COL_BLOCKS]
        product = jnp.einsum('kij,kif->kjf', values, picked, precision=lax.Precision.HIGHEST)
        product = product * live[:, None, None]
        partial_value = jax.ops.segment_sum(product, tile_ids % COL_BLOCKS, num_segments=COL_BLOCKS)
        partial_value = partial_value.reshape(tile_cols, HIDDEN_SIZE)
        start = (grid_c * tile_cols).astype(jnp.int32)
        current = lax.dynamic_slice_in_dim(total, start, tile_cols, 0)
        return lax.dynamic_update_slice_in_dim(total, current + partial_value, start, 0)
    grad_cluster = lax.fori_loop(0, grid_total, backward_tile, jnp.zeros((NODES, HIDDEN_SIZE), jnp.float32))
    rounded = grad_cluster.astype(jnp.bfloat16).reshape(grid_total, NODES_DEV, HIDDEN_SIZE)
    ordered = jnp.take_along_axis(rounded, node_perm[:, :, None], axis=1)
    return (ordered.reshape(NODES, HIDDEN_SIZE), weight_grad)
```

```python
import math

import jax
import jax.numpy as jnp
from jax import lax
from jax.experimental import pallas as pl
from jax.experimental.pallas import tpu as pltpu
from jax.sharding import PartitionSpec as P

BLOCK = 128
HIDDEN = 128
YL, C, X, YH = 2, 2, 4, 4
CHUNK = 8
MESH = pl.DeviceIdType.MESH
F32, BF16 = jnp.float32, jnp.bfloat16
VMEM = pl.BlockSpec(memory_space=pltpu.VMEM)
SMEM = pl.BlockSpec(memory_space=pltpu.SMEM)
HBM = pl.BlockSpec(memory_space=pl.ANY)


def far_first(n):
    return sorted(range(1, n), key=lambda d: (-min(d, n - d), d))


def near_first(n):
    return sorted(range(1, n), key=lambda d: (min(d, n - d), d))


def remote(src, dst, send, recv, device):
    return pltpu.make_async_remote_copy(
        src_ref=src, dst_ref=dst, send_sem=send, recv_sem=recv, device_id=device, device_id_type=MESH
    )


def greet(devices):
    barrier = pltpu.get_barrier_semaphore()
    for device in devices:
        pl.semaphore_signal(barrier, inc=1, device_id=device, device_id_type=MESH)
    pl.semaphore_wait(barrier, len(devices))


def gather_features(x_ref, out_ref, zs, zr, ys, yr):
    r, c = lax.axis_index("row"), lax.axis_index("col")
    nz = out_ref.shape[0] // YL
    z, y = r // YL, r % YL
    side = (z * YL + 1 - y, c)

    def other(d):
        return ((z + d) % nz * YL + y, c)

    def came(d):
        return (z + nz - d) % nz * YL + y

    greet([side] + [other(d) for d in range(1, nz)])
    sends = []
    for d in near_first(nz):
        copy = remote(x_ref, out_ref.at[r], zs.at[d], zr.at[d], other(d))
        copy.start()
        sends.append(copy)
    copy = remote(x_ref, out_ref.at[r], ys.at[0], yr.at[0], side)
    copy.start()
    sends.append(copy)
    out_ref[r] = x_ref[...]
    for d in near_first(nz):
        at = came(d)
        remote(x_ref, out_ref.at[at], zs.at[d], zr.at[d], other(d)).wait_recv()
        copy = remote(out_ref.at[at], out_ref.at[at], ys.at[d], yr.at[d], side)
        copy.start()
        sends.append(copy)
    for d in range(nz):
        at = (z + nz - d) % nz * YL + 1 - y
        remote(x_ref, out_ref.at[at], ys.at[d], yr.at[d], side).wait_recv()
    for copy in sends:
        copy.wait_send()


def spmm(ids_ref, count_ref, vals_ref, src_ref, out_ref, acc, vbuf, sems, *, cols, forward):
    count = count_ref[0, 0]
    chunks = (count + CHUNK - 1) // CHUNK
    dead = acc.shape[0] - 1

    def fetch(j):
        at = pl.ds(j * CHUNK, CHUNK)
        return pltpu.make_async_copy(vals_ref.at[at], vbuf.at[at], sems.at[j])

    lax.fori_loop(0, chunks, lambda j, _: (fetch(j).start(), 0)[1], 0)
    acc[...] = jnp.zeros_like(acc)

    def step(j, _):
        fetch(j).wait()
        for half in range(0, CHUNK, 4):
            made = []
            for i in range(4):
                k = j * CHUNK + half + i
                where = ids_ref[0, k]
                p, q = where // cols, where % cols
                if forward:
                    got = jnp.dot(vbuf[k], src_ref[q], preferred_element_type=F32)
                    to = p
                else:
                    got = jnp.dot(
                        src_ref[p % C * (src_ref.shape[0] // C) + p // C],
                        vbuf[k],
                        preferred_element_type=F32,
                    )
                    to = q
                made.append((jnp.where(k < count, to, dead), got))
            for to, got in made:
                acc[to] = acc[to] + got
        return 0

    lax.fori_loop(0, chunks, step, 0)
    fast = C if forward else YL
    for b in range(dead):
        out_ref[b % fast * (dead // fast) + b // fast] = acc[b].astype(BF16)


def reduce_and_step(
    part, grad_ref, w_ref, out_ref, wsum_ref,
    sib, sx, rx, sy, ry, share, wpart, wsib, wmine, wx, wy,
    cs, cr, xs, xr, hs, hr, gys, gyr, gxs, gxr, gcs, gcr, wcs, wcr, wxs, wxr, wys, wyr,
):
    r, c = lax.axis_index("row"), lax.axis_index("col")
    core = c % C
    x, h = c // C // YH, c // C % YH
    side = (r, (x * YH + h) * C + 1 - core)

    def at_x(d):
        return (r, ((x + d) % X * YH + h) * C + core)

    def at_h(d):
        return (r, (x * YH + (h + d) % YH) * C + core)

    greet([side] + [at_x(d) for d in range(1, X)] + [at_h(d) for d in range(1, YH)])
    sends = []

    def send(*args):
        copy = remote(*args)
        copy.start()
        sends.append(copy)

    for d in far_first(X) + [0]:
        to = (x + d) % X
        send(part.at[1 - core, to], sib.at[to], cs.at[d], cr.at[d], side)
    for d in far_first(X):
        to = (x + d) % X
        remote(part.at[core, to], sib.at[to], cs.at[d], cr.at[d], side).wait_recv()
        sx[to] = (part[core, to].astype(F32) + sib[to].astype(F32)).astype(BF16)
        send(sx.at[to], rx.at[x], xs.at[d], xr.at[d], at_x(d))
    remote(part.at[core, x], sib.at[x], cs.at[0], cr.at[0], side).wait_recv()
    for d in near_first(X):
        frm = (x + X - d) % X
        remote(sx.at[frm], rx.at[frm], xs.at[d], xr.at[d], at_x(d)).wait_recv()

    def summed(to):
        total = part[core, x, to].astype(F32) + sib[x, to].astype(F32)
        for d in range(1, X):
            total = total + rx[(x + d) % X, to].astype(F32)
        return total

    for d in far_first(YH):
        to = (h + d) % YH
        sy[to] = summed(to).astype(BF16)
        send(sy.at[to], ry.at[h], hs.at[d], hr.at[d], at_h(d))
    aggregate = summed(h)
    for d in near_first(YH):
        frm = (h + YH - d) % YH
        remote(sy.at[frm], ry.at[frm], hs.at[d], hr.at[d], at_h(d)).wait_recv()
    for d in range(1, YH):
        aggregate = aggregate + ry[(h + d) % YH].astype(F32)
    agg_low = aggregate.astype(BF16)
    weight = w_ref[...]
    pre = jnp.dot(agg_low, weight, preferred_element_type=F32)
    sigma = 1.0 / (1.0 + jnp.exp(-pre))
    grad_pre = (grad_ref[...].astype(F32) * sigma * (1.0 + pre * (1.0 - sigma))).astype(BF16)
    flipped = lax.dot_general(weight, grad_pre, (((1,), (1,)), ((), ())), preferred_element_type=F32)
    share[...] = flipped.astype(BF16)
    for d in far_first(YH):
        send(share, out_ref.at[core, x, h], gys.at[d], gyr.at[d], at_h(d))
    for d in far_first(X):
        send(share, out_ref.at[core, x, h], gxs.at[d, 0], gxr.at[d, 0], at_x(d))
    send(share, out_ref.at[core, x, h], gcs.at[0, 0], gcr.at[0, 0], side)
    out_ref[core, x, h] = flipped.astype(BF16)

    half, piece = BLOCK // C, BLOCK // C // X
    wpart[...] = lax.dot_general(
        agg_low, grad_pre, (((0,), (0,)), ((), ())), preferred_element_type=F32
    ).reshape(C, half, HIDDEN)
    send(wpart.at[1 - core], wsib, wcs, wcr, side)
    remote(wpart.at[core], wsib, wcs, wcr, side).wait_recv()
    wmine[...] = (wpart[core] + wsib[...]).reshape(X, piece, HIDDEN)
    for d in far_first(X):
        send(wmine.at[(x + d) % X], wx.at[x], wxs.at[d], wxr.at[d], at_x(d))
    wx[x] = wmine[x]

    for d in near_first(YH):
        block = out_ref.at[core, x, (h + YH - d) % YH]
        remote(share, block, gys.at[d], gyr.at[d], at_h(d)).wait_recv()
        for e in far_first(X):
            send(block, block, gxs.at[e, d], gxr.at[e, d], at_x(e))
        send(block, block, gcs.at[0, d], gcr.at[0, d], side)

    for d in near_first(X):
        frm = (x + X - d) % X
        remote(wmine.at[frm], wx.at[frm], wxs.at[d], wxr.at[d], at_x(d)).wait_recv()
    total = wx[0]
    for s in range(1, X):
        total = total + wx[s]
    wy[h] = total
    for d in far_first(YH):
        send(wy.at[h], wy.at[h], wys.at[d], wyr.at[d], at_h(d))

    for d in [0] + near_first(YH):
        for e in near_first(X):
            block = out_ref.at[core, (x + X - e) % X, (h + YH - d) % YH]
            remote(share, block, gxs.at[e, d], gxr.at[e, d], at_x(e)).wait_recv()
            send(block, block, gcs.at[e, d], gcr.at[e, d], side)

    for d in near_first(YH):
        frm = (h + YH - d) % YH
        remote(wy.at[frm], wy.at[frm], wys.at[d], wyr.at[d], at_h(d)).wait_recv()
    total = wy[0]
    for s in range(1, YH):
        total = total + wy[s]
    wsum_ref[...] = total

    for d in range(YH):
        for e in range(X):
            block = out_ref.at[1 - core, (x + X - e) % X, (h + YH - d) % YH]
            remote(share, block, gcs.at[e, d], gcr.at[e, d], side).wait_recv()
    for copy in sends:
        copy.wait_send()


def reduce_and_order(
    part, perm_ref, wsum_ref, out_ref, wout_ref,
    sib, sz, rz, wside, wz, wall,
    ys, yr, zs, zr, wys, wyr, wzs, wzr, wxs, wxr, wcs, wcr,
    *, scale,
):
    r, c = lax.axis_index("row"), lax.axis_index("col")
    nz = part.shape[1]
    z, y = r // YL, r % YL
    core = c % C
    x, h = c // C // YH, c // C % YH
    side_y = (z * YL + 1 - y, c)
    side_c = (r, (x * YH + h) * C + 1 - core)

    def at_z(d):
        return ((z + d) % nz * YL + y, c)

    def at_x(d):
        return (r, ((x + d) % X * YH + h) * C + core)

    greet(
        [side_y, side_c] + [at_z(d) for d in range(1, nz)] + [at_x(d) for d in range(1, X)]
    )
    sends = []

    def send(*args):
        copy = remote(*args)
        copy.start()
        sends.append(copy)

    send(wsum_ref, wside, wys, wyr, side_y)
    for d in far_first(nz) + [0]:
        to = (z + d) % nz
        send(part.at[1 - y, to], sib.at[to], ys.at[d], yr.at[d], side_y)
    remote(wsum_ref, wside, wys, wyr, side_y).wait_recv()
    wz[z] = wsum_ref[...] + wside[...]
    for d in far_first(nz):
        send(wz.at[z], wz.at[z], wzs.at[d], wzr.at[d], at_z(d))
    for d in far_first(nz):
        to = (z + d) % nz
        remote(part.at[y, to], sib.at[to], ys.at[d], yr.at[d], side_y).wait_recv()
        sz[to] = (part[y, to].astype(F32) + sib[to].astype(F32)).astype(BF16)
        send(sz.at[to], rz.at[z], zs.at[d], zr.at[d], at_z(d))
    remote(part.at[y, z], sib.at[z], ys.at[0], yr.at[0], side_y).wait_recv()
    grad = part[y, z].astype(F32) + sib[z].astype(F32)

    for d in near_first(nz):
        frm = (z + nz - d) % nz
        remote(wz.at[frm], wz.at[frm], wzs.at[d], wzr.at[d], at_z(d)).wait_recv()
    total = wz[0]
    for s in range(1, nz):
        total = total + wz[s]
    wall[core, x] = total * scale
    for d in far_first(X):
        send(wall.at[core, x], wall.at[core, x], wxs.at[d], wxr.at[d], at_x(d))
    for d in near_first(X):
        block = wall.at[core, (x + X - d) % X]
        remote(block, block, wxs.at[d], wxr.at[d], at_x(d)).wait_recv()
    send(wall.at[core], wall.at[core], wcs, wcr, side_c)

    for d in near_first(nz):
        frm = (z + nz - d) % nz
        remote(sz.at[frm], rz.at[frm], zs.at[d], zr.at[d], at_z(d)).wait_recv()
        grad = grad + rz[frm].astype(F32)
    hot = lax.broadcasted_iota(jnp.int32, (BLOCK, BLOCK), 0) == perm_ref[...]
    hot = jnp.where(hot, 1.0, 0.0).astype(BF16)
    moved = jnp.dot(grad.astype(BF16), hot, preferred_element_type=F32)
    out_ref[...] = moved.T.astype(BF16)
    remote(wall.at[1 - core], wall.at[1 - core], wcs, wcr, side_c).wait_recv()
    wout_ref[...] = wall[...].reshape(BLOCK, HIDDEN)
    for copy in sends:
        copy.wait_send()


def dma(*shape):
    return pltpu.SemaphoreType.DMA(shape) if shape else pltpu.SemaphoreType.DMA


def shards(features, grad_out, weight, block_ids, block_vals, block_count, node_perm):
    rows, cols = lax.axis_size("row"), lax.axis_size("col")
    nz = rows // YL
    slots = block_ids.shape[-1]
    blk = (BLOCK, HIDDEN)
    ids, vals = block_ids[0], block_vals[0, 0]
    piece = BLOCK // C // X

    source = pl.pallas_call(
        gather_features,
        out_shape=jax.ShapeDtypeStruct((rows,) + blk, BF16),
        in_specs=[VMEM],
        out_specs=VMEM,
        scratch_shapes=[dma(nz), dma(nz), dma(nz), dma(nz)],
        compiler_params=pltpu.CompilerParams(collective_id=0, has_side_effects=True),
        name="gather_features",
    )(features)

    def multiply(src, targets, forward, name):
        return pl.pallas_call(
            lambda *refs: spmm(*refs, cols=rows, forward=forward),
            out_shape=jax.ShapeDtypeStruct((targets,) + blk, BF16),
            in_specs=[SMEM, SMEM, HBM, VMEM],
            out_specs=VMEM,
            scratch_shapes=[
                pltpu.VMEM((targets + 1,) + blk, F32),
                pltpu.VMEM((slots,) + blk, BF16),
                dma(slots // CHUNK),
            ],
            name=name,
        )(ids, block_count, vals, src)

    part = multiply(source, cols, True, "aggregate").reshape((C, X, YH) + blk)
    grads, wsum = pl.pallas_call(
        reduce_and_step,
        out_shape=(
            jax.ShapeDtypeStruct((C, X, YH) + blk, BF16),
            jax.ShapeDtypeStruct((piece, HIDDEN), F32),
        ),
        in_specs=[VMEM] * 3,
        out_specs=(VMEM, VMEM),
        scratch_shapes=[
            pltpu.VMEM((X, YH) + blk, BF16),
            pltpu.VMEM((X, YH) + blk, BF16),
            pltpu.VMEM((X, YH) + blk, BF16),
            pltpu.VMEM((YH,) + blk, BF16),
            pltpu.VMEM((YH,) + blk, BF16),
            pltpu.VMEM(blk, BF16),
            pltpu.VMEM((C, BLOCK // C, HIDDEN), F32),
            pltpu.VMEM((BLOCK // C, HIDDEN), F32),
            pltpu.VMEM((X, piece, HIDDEN), F32),
            pltpu.VMEM((X, piece, HIDDEN), F32),
            pltpu.VMEM((YH, piece, HIDDEN), F32),
            dma(X), dma(X), dma(X), dma(X), dma(YH), dma(YH),
            dma(YH), dma(YH), dma(X, YH), dma(X, YH), dma(X, YH), dma(X, YH),
            dma(), dma(), dma(X), dma(X), dma(YH), dma(YH),
        ],
        compiler_params=pltpu.CompilerParams(collective_id=1, has_side_effects=True),
        name="reduce_and_step",
    )(part, grad_out, weight)
    back = multiply(grads.reshape((cols,) + blk), rows, False, "aggregate_back")
    scale = 1.0 / math.sqrt(rows * cols * BLOCK)
    return pl.pallas_call(
        lambda *refs: reduce_and_order(*refs, scale=scale),
        out_shape=(jax.ShapeDtypeStruct(blk, BF16), jax.ShapeDtypeStruct((BLOCK, HIDDEN), F32)),
        in_specs=[VMEM] * 3,
        out_specs=(VMEM, VMEM),
        scratch_shapes=[
            pltpu.VMEM((nz,) + blk, BF16),
            pltpu.VMEM((nz,) + blk, BF16),
            pltpu.VMEM((nz,) + blk, BF16),
            pltpu.VMEM((piece, HIDDEN), F32),
            pltpu.VMEM((nz, piece, HIDDEN), F32),
            pltpu.VMEM((C, X, piece, HIDDEN), F32),
            dma(nz), dma(nz), dma(nz), dma(nz), dma(), dma(),
            dma(nz), dma(nz), dma(X), dma(X), dma(), dma(),
        ],
        compiler_params=pltpu.CompilerParams(collective_id=2, has_side_effects=True),
        name="reduce_and_order",
    )(back.reshape((YL, nz) + blk), node_perm, wsum)


def solution(mesh):
    in_specs = (
        P(("col", "row"), None),
        P(("row", "col"), None),
        P(),
        P("row", "col", None),
        P("row", "col", None, None, None),
        P("row", "col"),
        P(("col", "row"), None),
    )
    out_specs = (P(("col", "row"), None), P())
    return jax.shard_map(shards, mesh=mesh, in_specs=in_specs, out_specs=out_specs, check_vma=False)
```

```python
import math

import jax
import jax.numpy as jnp
from jax import lax
from jax.experimental import pallas as pl
from jax.experimental.pallas import tpu as pltpu
from jax.sharding import PartitionSpec as P

BLOCK = 128
HIDDEN = 128
YL, C, X, YH = 2, 2, 4, 4
CHUNK = 8
LIMIT = 16 << 20
WIDE = 50_000_000
LONG = pl.CostEstimate(flops=0, bytes_accessed=50_000_000, transcendentals=0)
MESH = pl.DeviceIdType.MESH
F32, BF16 = jnp.float32, jnp.bfloat16
VMEM = pl.BlockSpec(memory_space=pltpu.VMEM)
SMEM = pl.BlockSpec(memory_space=pltpu.SMEM)
HBM = pl.BlockSpec(memory_space=pl.ANY)


def far_first(n):
    return sorted(range(1, n), key=lambda d: (-min(d, n - d), d))


def near_first(n):
    return sorted(range(1, n), key=lambda d: (min(d, n - d), d))


def remote(src, dst, send, recv, device):
    return pltpu.make_async_remote_copy(
        src_ref=src, dst_ref=dst, send_sem=send, recv_sem=recv, device_id=device, device_id_type=MESH
    )


def greet(devices):
    barrier = pltpu.get_barrier_semaphore()
    for device in devices:
        pl.semaphore_signal(barrier, inc=1, device_id=device, device_id_type=MESH)
    pl.semaphore_wait(barrier, len(devices))


def spread_along_z(z, nz, turn, at_z, slot, zs, zr, send):
    me = slot(z)
    for d in (2, nz - 2, 1, nz - 1):
        send(me, me, zs.at[d], zr.at[d], at_z(d))

    def arrive(d, sem):
        block = slot((z + nz - d) % nz)
        remote(block, block, zs.at[sem], zr.at[sem], at_z(d)).wait_recv()
        return block

    for d in (1, nz - 1):
        arrive(d, d)
        yield d
    for d in (2, nz - 2):
        block = arrive(d, d)
        onward = 1 if d == 2 else nz - 1
        send(block, block, zs.at[d + 1 if d == 2 else d - 1], zr.at[d + 1 if d == 2 else d - 1], at_z(onward))
        yield d
    back = slot((z + 2 * nz - 2 * turn) % nz)
    send(back, back, zs.at[4], zr.at[4], at_z(2 * nz + 2 * turn))
    for d in (3, nz - 3, 4):
        arrive(d, d)
        yield d


def gather_features(x_ref, vals_ref, out_ref, held_ref, zs, zr, ys, yr, loc, got):
    r, c = lax.axis_index("row"), lax.axis_index("col")
    nz = out_ref.shape[0] // YL
    z, y = r // YL, r % YL
    turn = 1 - 2 * (c % C)
    side = (z * YL + 1 - y, c)

    def at_z(d):
        return ((z + d) % nz * YL + y, c)

    own = pltpu.make_async_copy(x_ref, out_ref.at[r], loc)
    own.start()
    blocks = pltpu.make_async_copy(vals_ref, held_ref, got)
    blocks.start()
    greet([side] + [at_z(d) for d in (1, 2, nz - 2, nz - 1)])
    sends = []

    def send(*args):
        copy = remote(*args)
        copy.start()
        sends.append(copy)

    own.wait()
    send(out_ref.at[r], out_ref.at[r], ys.at[0], yr.at[0], side)
    for d in spread_along_z(z, nz, turn, at_z, lambda at: out_ref.at[at * YL + y], zs, zr, send):
        block = out_ref.at[(z + nz - d) % nz * YL + y]
        send(block, block, ys.at[d], yr.at[d], side)
    for d in range(nz):
        at = (z + nz - d) % nz * YL + 1 - y
        remote(x_ref, out_ref.at[at], ys.at[d], yr.at[d], side).wait_recv()
    for copy in sends:
        copy.wait_send()
    blocks.wait()


def spmm(ids_ref, count_ref, vals_ref, src_ref, out_ref, acc, *, cols, forward):
    count = count_ref[0, 0]
    chunks = (count + CHUNK - 1) // CHUNK
    dead = acc.shape[0] - 1

    acc[...] = jnp.zeros_like(acc)

    def step(j, _):
        for half in range(0, CHUNK, 4):
            made = []
            for i in range(4):
                k = j * CHUNK + half + i
                where = ids_ref[0, k]
                p, q = where // cols, where % cols
                if forward:
                    got = jnp.dot(vals_ref[k], src_ref[q], preferred_element_type=F32)
                    to = p
                else:
                    got = jnp.dot(
                        src_ref[p % C * (src_ref.shape[0] // C) + p // C],
                        vals_ref[k],
                        preferred_element_type=F32,
                    )
                    to = q
                made.append((jnp.where(k < count, to, dead), got))
            for to, got in made:
                acc[to] = acc[to] + got
        return 0

    lax.fori_loop(0, chunks, step, 0)
    fast = C if forward else YL
    for b in range(dead):
        out_ref[b % fast * (dead // fast) + b // fast] = acc[b].astype(BF16)


def reduce_and_step(
    part_ref, grad_ref, w_ref, out_ref, wsum_ref,
    part, sib, sx, rel, rx, sy, ry, share, wpart, wsib, wmine, wx, wy, loc,
    cs, cr, rs, rr, xs, xr, hs, hr, gys, gyr, gxs, gxr, gcs, gcr, wcs, wcr, wxs, wxr, wys, wyr,
):
    r, c = lax.axis_index("row"), lax.axis_index("col")
    core = c % C
    x, h = c // C // YH, c // C % YH
    side = (r, (x * YH + h) * C + 1 - core)

    def at_x(d):
        return (r, ((x + d) % X * YH + h) * C + core)

    def at_h(d):
        return (r, (x * YH + (h + d) % YH) * C + core)

    mine = pltpu.make_async_copy(part_ref.at[core], part, loc)
    mine.start()
    greet([side] + [at_x(d) for d in range(1, X)] + [at_h(d) for d in range(1, YH)])
    sends = []

    def send(*args):
        copy = remote(*args)
        copy.start()
        sends.append(copy)

    def at(e):
        return (h + e) % YH

    for d in (2, 1, 3, 0):
        to = (x + d) % X
        send(part_ref.at[1 - core, to], sib.at[to], cs.at[d], cr.at[d], side)
    mine.wait()

    def have(d):
        to = (x + d) % X
        remote(part.at[to], sib.at[to], cs.at[d], cr.at[d], side).wait_recv()

    def pair(d, e):
        to = (x + d) % X
        return part[to, at(e)].astype(F32) + sib[to, at(e)].astype(F32)

    def push(d, e, total):
        to = (x + d) % X
        sx[to, at(e)] = total.astype(BF16)
        n = 0 if d == 1 else 1
        send(sx.at[to, at(e)], rx.at[n, at(e)], xs.at[n, e], xr.at[n, e], at_x(d))

    ahead = {2: 1, 0: 1, 1: X - 1, 3: X - 1}
    order = (2, 1, 3, 0)
    have(2)
    for e in order:
        sx[(x + 2) % X, at(e)] = pair(2, e).astype(BF16)
        send(sx.at[(x + 2) % X, at(e)], rel.at[at(e)], rs.at[e], rr.at[e], at_x(ahead[e]))
    for d in (1, X - 1):
        have(d)
        for e in order:
            if ahead[e] != d:
                push(d, e, pair(d, e))
    for e in order:
        remote(sx.at[x, at(e)], rel.at[at(e)], rs.at[e], rr.at[e], at_x(1)).wait_recv()
        push(ahead[e], e, pair(ahead[e], e) + rel[at(e)].astype(F32))
    have(0)

    def summed(e):
        for n in (0, 1):
            remote(share, rx.at[n, at(e)], xs.at[n, e], xr.at[n, e], at_x(1)).wait_recv()
        return pair(0, e) + (rx[0, at(e)].astype(F32) + rx[1, at(e)].astype(F32))

    for d in (2, 1, 3):
        to = at(d)
        sy[to] = summed(d).astype(BF16)
        send(sy.at[to], ry.at[h], hs.at[d], hr.at[d], at_h(d))
    aggregate = summed(0)
    for d in near_first(YH):
        frm = (h + YH - d) % YH
        remote(sy.at[frm], ry.at[frm], hs.at[d], hr.at[d], at_h(d)).wait_recv()
    for d in range(1, YH):
        aggregate = aggregate + ry[(h + d) % YH].astype(F32)
    agg_low = aggregate.astype(BF16)
    weight = w_ref[...]
    pre = jnp.dot(agg_low, weight, preferred_element_type=F32)
    sigma = 1.0 / (1.0 + jnp.exp(-pre))
    grad_pre = (grad_ref[...].astype(F32) * sigma * (1.0 + pre * (1.0 - sigma))).astype(BF16)
    flipped = lax.dot_general(weight, grad_pre, (((1,), (1,)), ((), ())), preferred_element_type=F32)
    share[...] = flipped.astype(BF16)
    for d in far_first(YH):
        send(share, out_ref.at[core, x, h], gys.at[d], gyr.at[d], at_h(d))
    for d in (1, X - 1):
        send(share, out_ref.at[core, x, h], gxs.at[d, 0], gxr.at[d, 0], at_x(d))
    send(share, out_ref.at[core, x, h], gcs.at[0, 0], gcr.at[0, 0], side)
    out_ref[core, x, h] = flipped.astype(BF16)

    half, piece = BLOCK // C, BLOCK // C // X
    wpart[...] = lax.dot_general(
        agg_low, grad_pre, (((0,), (0,)), ((), ())), preferred_element_type=F32
    ).reshape(C, half, HIDDEN)
    send(wpart.at[1 - core], wsib, wcs, wcr, side)
    remote(wpart.at[core], wsib, wcs, wcr, side).wait_recv()
    wmine[...] = (wpart[core] + wsib[...]).reshape(X, piece, HIDDEN)
    for d in far_first(X):
        send(wmine.at[(x + d) % X], wx.at[x], wxs.at[d], wxr.at[d], at_x(d))
    wx[x] = wmine[x]

    for d in near_first(YH):
        block = out_ref.at[core, x, (h + YH - d) % YH]
        remote(share, block, gys.at[d], gyr.at[d], at_h(d)).wait_recv()
        for e in (1, X - 1):
            send(block, block, gxs.at[e, d], gxr.at[e, d], at_x(e))
        send(block, block, gcs.at[0, d], gcr.at[0, d], side)

    for d in near_first(X):
        frm = (x + X - d) % X
        remote(wmine.at[frm], wx.at[frm], wxs.at[d], wxr.at[d], at_x(d)).wait_recv()
    total = wx[0]
    for s in range(1, X):
        total = total + wx[s]
    wy[h] = total
    for d in far_first(YH):
        send(wy.at[h], wy.at[h], wys.at[d], wyr.at[d], at_h(d))

    for e in (1, X - 1, 2):
        for d in [0] + near_first(YH):
            block = out_ref.at[core, (x + X - e) % X, (h + YH - d) % YH]
            remote(share, block, gxs.at[e, d], gxr.at[e, d], at_x(e)).wait_recv()
            if e == ahead[d]:
                send(block, block, gxs.at[2, d], gxr.at[2, d], at_x(e))
            send(block, block, gcs.at[e, d], gcr.at[e, d], side)

    for d in near_first(YH):
        frm = (h + YH - d) % YH
        remote(wy.at[frm], wy.at[frm], wys.at[d], wyr.at[d], at_h(d)).wait_recv()
    total = wy[0]
    for s in range(1, YH):
        total = total + wy[s]
    wsum_ref[...] = total

    for d in range(YH):
        for e in range(X):
            block = out_ref.at[1 - core, (x + X - e) % X, (h + YH - d) % YH]
            remote(share, block, gcs.at[e, d], gcr.at[e, d], side).wait_recv()
    for copy in sends:
        copy.wait_send()


def reduce_and_order(
    part_ref, perm_ref, wsum_ref, out_ref, wout_ref,
    part, sib, sz, rel, far, rz, wside, wz, wall, loc,
    ys, yr, rs, rr, fs, fr, zs, zr, wys, wyr, wzs, wzr, wxs, wxr, wcs, wcr,
    *, scale,
):
    r, c = lax.axis_index("row"), lax.axis_index("col")
    nz = part_ref.shape[1]
    z, y = r // YL, r % YL
    core = c % C
    turn = 1 - 2 * core
    x, h = c // C // YH, c // C % YH
    side_y = (z * YL + 1 - y, c)
    side_c = (r, (x * YH + h) * C + 1 - core)

    def at_z(d):
        return ((z + d) % nz * YL + y, c)

    def at_x(d):
        return (r, ((x + d) % X * YH + h) * C + core)

    mine = pltpu.make_async_copy(part_ref.at[y], part, loc)
    mine.start()
    greet(
        [side_y, side_c]
        + [at_z(d) for d in (1, 2, nz - 2, nz - 1)]
        + [at_x(d) for d in range(1, X)]
    )
    sends = []

    def send(*args):
        copy = remote(*args)
        copy.start()
        sends.append(copy)

    send(wsum_ref, wside, wys, wyr, side_y)
    for d in far_first(nz) + [0]:
        to = (z + d) % nz
        send(part_ref.at[1 - y, to], sib.at[to], ys.at[d], yr.at[d], side_y)
    mine.wait()
    remote(wsum_ref, wside, wys, wyr, side_y).wait_recv()
    wz[z] = wsum_ref[...] + wside[...]
    spread = spread_along_z(z, nz, turn, at_z, lambda at: wz.at[at], wzs, wzr, send)
    next(spread)

    def pair(d):
        to = (z + d) % nz
        remote(part.at[to], sib.at[to], ys.at[d], yr.at[d], side_y).wait_recv()
        return part[to].astype(F32) + sib[to].astype(F32)

    def push(d, total, dst, ssem, rsem, device):
        to = (z + d) % nz
        sz[to] = total.astype(BF16)
        send(sz.at[to], dst, ssem, rsem, device)

    push(4, pair(4), far, fs, fr, at_z(2 * nz + 2 * turn))
    for n, d in ((0, 3), (1, nz - 3)):
        push(d, pair(d), rel.at[n], rs.at[n], rr.at[n], at_z(1 if n == 0 else nz - 1))
    two = [pair(2), pair(nz - 2)]
    for n, d in ((2, 1), (3, nz - 1)):
        push(d, pair(d), rz.at[n], zs.at[n], zr.at[n], at_z(d))
    grad = pair(0)
    remote(far, far, fs, fr, side_y).wait_recv()
    beyond = far[...].astype(F32)
    for n, d in ((0, 2), (1, nz - 2)):
        remote(rel.at[n], rel.at[n], rs.at[n], rr.at[n], side_y).wait_recv()
        total = two[n] + rel[n].astype(F32)
        total = total + jnp.where(core == n, beyond, 0.0)
        push(d, total, rz.at[n], zs.at[n], zr.at[n], at_z(d))

    for _ in spread:
        pass
    total = wz[0]
    for s in range(1, nz):
        total = total + wz[s]
    wall[core, x] = total * scale
    for d in far_first(X):
        send(wall.at[core, x], wall.at[core, x], wxs.at[d], wxr.at[d], at_x(d))
    for d in near_first(X):
        block = wall.at[core, (x + X - d) % X]
        remote(block, block, wxs.at[d], wxr.at[d], at_x(d)).wait_recv()
    send(wall.at[core], wall.at[core], wcs, wcr, side_c)

    for n in (2, 3, 0, 1):
        remote(rz.at[n], rz.at[n], zs.at[n], zr.at[n], side_y).wait_recv()
        grad = grad + rz[n].astype(F32)
    hot = lax.broadcasted_iota(jnp.int32, (BLOCK, BLOCK), 0) == perm_ref[...]
    hot = jnp.where(hot, 1.0, 0.0).astype(BF16)
    moved = jnp.dot(grad.astype(BF16), hot, preferred_element_type=F32)
    out_ref[...] = moved.T.astype(BF16)
    remote(wall.at[1 - core], wall.at[1 - core], wcs, wcr, side_c).wait_recv()
    wout_ref[...] = wall[...].reshape(BLOCK, HIDDEN)
    for copy in sends:
        copy.wait_send()


def dma(*shape):
    return pltpu.SemaphoreType.DMA(shape) if shape else pltpu.SemaphoreType.DMA


def shards(features, grad_out, weight, block_ids, block_vals, block_count, node_perm):
    rows, cols = lax.axis_size("row"), lax.axis_size("col")
    nz = rows // YL
    blk = (BLOCK, HIDDEN)
    ids = block_ids[0]
    piece = BLOCK // C // X

    source, vals = pl.pallas_call(
        gather_features,
        out_shape=(
            jax.ShapeDtypeStruct((rows,) + blk, BF16),
            jax.ShapeDtypeStruct(block_vals.shape[2:], BF16),
        ),
        in_specs=[VMEM, pl.BlockSpec(memory_space=pltpu.HBM)],
        out_specs=(VMEM, VMEM),
        scratch_shapes=[dma(nz), dma(nz), dma(nz), dma(nz), dma(), dma()],
        compiler_params=pltpu.CompilerParams(collective_id=0, has_side_effects=True, vmem_limit_bytes=WIDE),
        cost_estimate=LONG,
        name="gather_features",
    )(features, block_vals[0, 0])

    def multiply(src, targets, forward, name):
        return pl.pallas_call(
            lambda *refs: spmm(*refs, cols=rows, forward=forward),
            out_shape=jax.ShapeDtypeStruct((targets,) + blk, BF16),
            in_specs=[SMEM, SMEM, VMEM, VMEM],
            out_specs=VMEM,
            scratch_shapes=[
                pltpu.VMEM((targets + 1,) + blk, F32),
            ],
            compiler_params=pltpu.CompilerParams(vmem_limit_bytes=LIMIT),
            name=name,
        )(ids, block_count, vals, src)

    part = multiply(source, cols, True, "aggregate").reshape((C, X, YH) + blk)
    grads, wsum = pl.pallas_call(
        reduce_and_step,
        out_shape=(
            jax.ShapeDtypeStruct((C, X, YH) + blk, BF16),
            jax.ShapeDtypeStruct((piece, HIDDEN), F32),
        ),
        in_specs=[HBM, VMEM, VMEM],
        out_specs=(VMEM, VMEM),
        scratch_shapes=[
            pltpu.VMEM((X, YH) + blk, BF16),
            pltpu.VMEM((X, YH) + blk, BF16),
            pltpu.VMEM((X, YH) + blk, BF16),
            pltpu.VMEM((YH,) + blk, BF16),
            pltpu.VMEM((2, YH) + blk, BF16),
            pltpu.VMEM((YH,) + blk, BF16),
            pltpu.VMEM((YH,) + blk, BF16),
            pltpu.VMEM(blk, BF16),
            pltpu.VMEM((C, BLOCK // C, HIDDEN), F32),
            pltpu.VMEM((BLOCK // C, HIDDEN), F32),
            pltpu.VMEM((X, piece, HIDDEN), F32),
            pltpu.VMEM((X, piece, HIDDEN), F32),
            pltpu.VMEM((YH, piece, HIDDEN), F32),
            dma(),
            dma(X), dma(X), dma(YH), dma(YH), dma(2, YH), dma(2, YH), dma(YH), dma(YH),
            dma(YH), dma(YH), dma(X, YH), dma(X, YH), dma(X, YH), dma(X, YH),
            dma(), dma(), dma(X), dma(X), dma(YH), dma(YH),
        ],
        compiler_params=pltpu.CompilerParams(collective_id=1, has_side_effects=True, vmem_limit_bytes=LIMIT),
        cost_estimate=LONG,
        name="reduce_and_step",
    )(part, grad_out, weight)
    back = multiply(grads.reshape((cols,) + blk), rows, False, "aggregate_back")
    scale = 1.0 / math.sqrt(rows * cols * BLOCK)
    return pl.pallas_call(
        lambda *refs: reduce_and_order(*refs, scale=scale),
        out_shape=(jax.ShapeDtypeStruct(blk, BF16), jax.ShapeDtypeStruct((BLOCK, HIDDEN), F32)),
        in_specs=[HBM, VMEM, VMEM],
        out_specs=(VMEM, VMEM),
        scratch_shapes=[
            pltpu.VMEM((nz,) + blk, BF16),
            pltpu.VMEM((nz,) + blk, BF16),
            pltpu.VMEM((nz,) + blk, BF16),
            pltpu.VMEM((2,) + blk, BF16),
            pltpu.VMEM(blk, BF16),
            pltpu.VMEM((4,) + blk, BF16),
            pltpu.VMEM((piece, HIDDEN), F32),
            pltpu.VMEM((nz, piece, HIDDEN), F32),
            pltpu.VMEM((C, X, piece, HIDDEN), F32),
            dma(),
            dma(nz), dma(nz), dma(2), dma(2), dma(), dma(), dma(4), dma(4), dma(), dma(),
            dma(nz), dma(nz), dma(X), dma(X), dma(), dma(),
        ],
        compiler_params=pltpu.CompilerParams(collective_id=2, has_side_effects=True, vmem_limit_bytes=LIMIT),
        cost_estimate=LONG,
        name="reduce_and_order",
    )(back.reshape((YL, nz) + blk), node_perm, wsum)


def solution(mesh):
    in_specs = (
        P(("col", "row"), None),
        P(("row", "col"), None),
        P(),
        P("row", "col", None),
        P("row", "col", None, None, None),
        P("row", "col"),
        P(("col", "row"), None),
    )
    out_specs = (P(("col", "row"), None), P())
    return jax.shard_map(shards, mesh=mesh, in_specs=in_specs, out_specs=out_specs, check_vma=False)
```

```python
import math

import jax
import jax.numpy as jnp
from jax import lax
from jax.experimental import pallas as pl
from jax.experimental.pallas import tpu as pltpu
from jax.sharding import PartitionSpec as P

BLOCK = 128
HIDDEN = 128
YL, C, X, YH = 2, 2, 4, 4
CHUNK = 8
LIMIT = 16 << 20
WIDE = 50_000_000
LONG = pl.CostEstimate(flops=0, bytes_accessed=50_000_000, transcendentals=0)
MESH = pl.DeviceIdType.MESH
F32, BF16 = jnp.float32, jnp.bfloat16
VMEM = pl.BlockSpec(memory_space=pltpu.VMEM)
SMEM = pl.BlockSpec(memory_space=pltpu.SMEM)
HBM = pl.BlockSpec(memory_space=pl.ANY)


def far_first(n):
    return sorted(range(1, n), key=lambda d: (-min(d, n - d), d))


def near_first(n):
    return sorted(range(1, n), key=lambda d: (min(d, n - d), d))


def remote(src, dst, send, recv, device):
    return pltpu.make_async_remote_copy(
        src_ref=src, dst_ref=dst, send_sem=send, recv_sem=recv, device_id=device, device_id_type=MESH
    )


def greet(devices):
    barrier = pltpu.get_barrier_semaphore()
    for device in devices:
        pl.semaphore_signal(barrier, inc=1, device_id=device, device_id_type=MESH)
    pl.semaphore_wait(barrier, len(devices))


def spread_along_z(z, nz, turn, at_z, slot, zs, zr, send):
    me = slot(z)
    for d in (2, nz - 2, 1, nz - 1):
        send(me, me, zs.at[d], zr.at[d], at_z(d))

    def arrive(d, sem):
        block = slot((z + nz - d) % nz)
        remote(block, block, zs.at[sem], zr.at[sem], at_z(d)).wait_recv()
        return block

    for d in (1, nz - 1):
        arrive(d, d)
        yield d
    for d in (2, nz - 2):
        block = arrive(d, d)
        onward = 1 if d == 2 else nz - 1
        send(block, block, zs.at[d + 1 if d == 2 else d - 1], zr.at[d + 1 if d == 2 else d - 1], at_z(onward))
        yield d
    back = slot((z + 2 * nz - 2 * turn) % nz)
    send(back, back, zs.at[4], zr.at[4], at_z(2 * nz + 2 * turn))
    for d in (3, nz - 3, 4):
        arrive(d, d)
        yield d


def gather_features(x_ref, vals_ref, out_ref, held_ref, zs, zr, ys, yr, loc, got):
    r, c = lax.axis_index("row"), lax.axis_index("col")
    nz = out_ref.shape[0] // YL
    z, y = r // YL, r % YL
    turn = 1 - 2 * (c % C)
    side = (z * YL + 1 - y, c)

    def at_z(d):
        return ((z + d) % nz * YL + y, c)

    own = pltpu.make_async_copy(x_ref, out_ref.at[r], loc)
    own.start()
    blocks = pltpu.make_async_copy(vals_ref, held_ref, got)
    blocks.start()
    greet([side] + [at_z(d) for d in (1, 2, nz - 2, nz - 1)])
    sends = []

    def send(*args):
        copy = remote(*args)
        copy.start()
        sends.append(copy)

    own.wait()
    send(out_ref.at[r], out_ref.at[r], ys.at[0], yr.at[0], side)
    for d in spread_along_z(z, nz, turn, at_z, lambda at: out_ref.at[at * YL + y], zs, zr, send):
        block = out_ref.at[(z + nz - d) % nz * YL + y]
        send(block, block, ys.at[d], yr.at[d], side)
    for d in range(nz):
        at = (z + nz - d) % nz * YL + 1 - y
        remote(x_ref, out_ref.at[at], ys.at[d], yr.at[d], side).wait_recv()
    for copy in sends:
        copy.wait_send()
    blocks.wait()


def spmm(ids_ref, count_ref, vals_ref, src_ref, out_ref, acc, *, cols, forward):
    count = count_ref[0, 0]
    chunks = (count + CHUNK - 1) // CHUNK
    dead = acc.shape[0] - 1

    acc[...] = jnp.zeros_like(acc)

    def step(j, _):
        for half in range(0, CHUNK, 4):
            made = []
            for i in range(4):
                k = j * CHUNK + half + i
                where = ids_ref[0, k]
                p, q = where // cols, where % cols
                if forward:
                    got = jnp.dot(vals_ref[k], src_ref[q], preferred_element_type=F32)
                    to = p
                else:
                    got = jnp.dot(
                        src_ref[p % C * (src_ref.shape[0] // C) + p // C],
                        vals_ref[k],
                        preferred_element_type=F32,
                    )
                    to = q
                made.append((jnp.where(k < count, to, dead), got))
            for to, got in made:
                acc[to] = acc[to] + got
        return 0

    lax.fori_loop(0, chunks, step, 0)
    fast = C if forward else YL
    for b in range(dead):
        out_ref[b % fast * (dead // fast) + b // fast] = acc[b].astype(BF16)


def reduce_and_step(
    part_ref, grad_ref, w_ref, out_ref, wsum_ref,
    part, sib, sx, rel, rx, sy, ry, share, wpart, wx, wy, loc,
    cs, cr, rs, rr, xs, xr, hs, hr, gys, gyr, gxs, gxr, gcs, gcr, wxs, wxr, wys, wyr,
):
    r, c = lax.axis_index("row"), lax.axis_index("col")
    core = c % C
    x, h = c // C // YH, c // C % YH
    side = (r, (x * YH + h) * C + 1 - core)

    def at_x(d):
        return (r, ((x + d) % X * YH + h) * C + core)

    def at_h(d):
        return (r, (x * YH + (h + d) % YH) * C + core)

    z, y = r // YL, r % YL

    def at_xc(f, d):
        return (r, ((x + d) % X * YH + h) * C + (core + f) % C)

    def at_yh(f, d):
        return (z * YL + (y + f) % YL, (x * YH + (h + d) % YH) * C + core)

    across = [(f, d) for f in range(C) for d in range(X) if f or d]
    along = [(f, d) for f in range(YL) for d in range(YH) if f or d]
    mine = pltpu.make_async_copy(part_ref.at[core], part, loc)
    mine.start()
    greet([at_xc(f, d) for f, d in across] + [at_yh(f, d) for f, d in along])
    sends = []

    def send(*args):
        copy = remote(*args)
        copy.start()
        sends.append(copy)

    def at(e):
        return (h + e) % YH

    for d in (2, 1, 3, 0):
        to = (x + d) % X
        send(part_ref.at[1 - core, to], sib.at[to], cs.at[d], cr.at[d], side)
    mine.wait()

    def have(d):
        to = (x + d) % X
        remote(part.at[to], sib.at[to], cs.at[d], cr.at[d], side).wait_recv()

    def pair(d, e):
        to = (x + d) % X
        return part[to, at(e)].astype(F32) + sib[to, at(e)].astype(F32)

    def push(d, e, total):
        to = (x + d) % X
        sx[to, at(e)] = total.astype(BF16)
        n = 0 if d == 1 else 1
        send(sx.at[to, at(e)], rx.at[n, at(e)], xs.at[n, e], xr.at[n, e], at_x(d))

    ahead = {2: 1, 0: 1, 1: X - 1, 3: X - 1}
    order = (2, 1, 3, 0)
    have(2)
    for e in order:
        sx[(x + 2) % X, at(e)] = pair(2, e).astype(BF16)
        send(sx.at[(x + 2) % X, at(e)], rel.at[at(e)], rs.at[e], rr.at[e], at_x(ahead[e]))
    for d in (1, X - 1):
        have(d)
        for e in order:
            if ahead[e] != d:
                push(d, e, pair(d, e))
    for e in order:
        remote(sx.at[x, at(e)], rel.at[at(e)], rs.at[e], rr.at[e], at_x(1)).wait_recv()
        push(ahead[e], e, pair(ahead[e], e) + rel[at(e)].astype(F32))
    have(0)

    def summed(e):
        for n in (0, 1):
            remote(share, rx.at[n, at(e)], xs.at[n, e], xr.at[n, e], at_x(1)).wait_recv()
        return pair(0, e) + (rx[0, at(e)].astype(F32) + rx[1, at(e)].astype(F32))

    for d in (2, 1, 3):
        to = at(d)
        sy[to] = summed(d).astype(BF16)
        send(sy.at[to], ry.at[h], hs.at[d], hr.at[d], at_h(d))
    aggregate = summed(0)
    for d in near_first(YH):
        frm = (h + YH - d) % YH
        remote(sy.at[frm], ry.at[frm], hs.at[d], hr.at[d], at_h(d)).wait_recv()
    for d in range(1, YH):
        aggregate = aggregate + ry[(h + d) % YH].astype(F32)
    agg_low = aggregate.astype(BF16)
    weight = w_ref[...]
    pre = jnp.dot(agg_low, weight, preferred_element_type=F32)
    sigma = 1.0 / (1.0 + jnp.exp(-pre))
    grad_pre = (grad_ref[...].astype(F32) * sigma * (1.0 + pre * (1.0 - sigma))).astype(BF16)
    flipped = lax.dot_general(weight, grad_pre, (((1,), (1,)), ((), ())), preferred_element_type=F32)
    share[...] = flipped.astype(BF16)
    for d in far_first(YH):
        send(share, out_ref.at[core, x, h], gys.at[d], gyr.at[d], at_h(d))
    for d in (1, X - 1):
        send(share, out_ref.at[core, x, h], gxs.at[d, 0], gxr.at[d, 0], at_x(d))
    send(share, out_ref.at[core, x, h], gcs.at[0, 0], gcr.at[0, 0], side)
    out_ref[core, x, h] = flipped.astype(BF16)

    wpart[...] = lax.dot_general(
        agg_low, grad_pre, (((0,), (0,)), ((), ())), preferred_element_type=F32
    ).reshape(wpart.shape)
    for f, d in across:
        piece = wpart.at[(core + f) % C, (x + d) % X]
        send(piece, wx.at[core, x], wxs.at[f, d], wxr.at[f, d], at_xc(f, d))
    wx[core, x] = wpart[core, x]

    for d in near_first(YH):
        block = out_ref.at[core, x, (h + YH - d) % YH]
        remote(share, block, gys.at[d], gyr.at[d], at_h(d)).wait_recv()
        for e in (1, X - 1):
            send(block, block, gxs.at[e, d], gxr.at[e, d], at_x(e))
        send(block, block, gcs.at[0, d], gcr.at[0, d], side)

    for f, d in across:
        came = wx.at[(core + f) % C, (x + X - d) % X]
        remote(came, came, wxs.at[f, d], wxr.at[f, d], at_xc(f, d)).wait_recv()
    total = wx[0, 0]
    for n in range(1, C * X):
        total = total + wx[n // X, n % X]
    wy[y, h] = total
    for f, d in along:
        send(wy.at[y, h], wy.at[y, h], wys.at[f, d], wyr.at[f, d], at_yh(f, d))

    for e in (1, X - 1, 2):
        for d in [0] + near_first(YH):
            block = out_ref.at[core, (x + X - e) % X, (h + YH - d) % YH]
            remote(share, block, gxs.at[e, d], gxr.at[e, d], at_x(e)).wait_recv()
            if e == ahead[d]:
                send(block, block, gxs.at[2, d], gxr.at[2, d], at_x(e))
            send(block, block, gcs.at[e, d], gcr.at[e, d], side)

    for f, d in along:
        came = wy.at[(y + f) % YL, (h + YH - d) % YH]
        remote(came, came, wys.at[f, d], wyr.at[f, d], at_yh(f, d)).wait_recv()
    total = wy[0, 0]
    for n in range(1, YL * YH):
        total = total + wy[n // YH, n % YH]
    wsum_ref[...] = total

    for d in range(YH):
        for e in range(X):
            block = out_ref.at[1 - core, (x + X - e) % X, (h + YH - d) % YH]
            remote(share, block, gcs.at[e, d], gcr.at[e, d], side).wait_recv()
    for copy in sends:
        copy.wait_send()


def reduce_and_order(
    part_ref, perm_ref, wsum_ref, out_ref, wout_ref,
    part, sib, sz, rz, wz, wall, loc,
    ys, yr, zs, zr, wzs, wzr, wxs, wxr,
    *, scale,
):
    r, c = lax.axis_index("row"), lax.axis_index("col")
    nz = part_ref.shape[1]
    z, y = r // YL, r % YL
    core = c % C
    x, h = c // C // YH, c // C % YH
    side = (z * YL + 1 - y, c)

    def at_z(d):
        return ((z + d) % nz * YL + y, c)

    def at_xc(f, d):
        return (r, ((x + d) % X * YH + h) * C + (core + f) % C)

    across = [(f, d) for f in range(C) for d in range(X) if f or d]
    mine = pltpu.make_async_copy(part_ref.at[y], part, loc)
    mine.start()
    greet([side] + [at_z(d) for d in range(1, nz)] + [at_xc(f, d) for f, d in across])
    sends = []

    def send(*args):
        copy = remote(*args)
        copy.start()
        sends.append(copy)

    for d in far_first(nz) + [0]:
        to = (z + d) % nz
        send(part_ref.at[1 - y, to], sib.at[to], ys.at[d], yr.at[d], side)
    for d in far_first(nz):
        send(wsum_ref, wz.at[z], wzs.at[d], wzr.at[d], at_z(d))
    wz[z] = wsum_ref[...]
    mine.wait()

    def pair(d):
        to = (z + d) % nz
        remote(part.at[to], sib.at[to], ys.at[d], yr.at[d], side).wait_recv()
        return part[to].astype(F32) + sib[to].astype(F32)

    for d in far_first(nz):
        to = (z + d) % nz
        sz[to] = pair(d).astype(BF16)
        send(sz.at[to], rz.at[z], zs.at[d], zr.at[d], at_z(d))
    grad = pair(0)

    for d in near_first(nz):
        came = wz.at[(z + nz - d) % nz]
        remote(came, came, wzs.at[d], wzr.at[d], at_z(d)).wait_recv()
    total = wz[0]
    for s in range(1, nz):
        total = total + wz[s]
    wall[core, x] = total * scale
    for f, d in across:
        send(wall.at[core, x], wall.at[core, x], wxs.at[f, d], wxr.at[f, d], at_xc(f, d))

    for d in near_first(nz):
        frm = (z + nz - d) % nz
        remote(sz.at[frm], rz.at[frm], zs.at[d], zr.at[d], at_z(d)).wait_recv()
        grad = grad + rz[frm].astype(F32)
    hot = lax.broadcasted_iota(jnp.int32, (BLOCK, BLOCK), 0) == perm_ref[...]
    hot = jnp.where(hot, 1.0, 0.0).astype(BF16)
    moved = jnp.dot(grad.astype(BF16), hot, preferred_element_type=F32)
    out_ref[...] = moved.T.astype(BF16)
    for f, d in across:
        came = wall.at[(core + f) % C, (x + X - d) % X]
        remote(came, came, wxs.at[f, d], wxr.at[f, d], at_xc(f, d)).wait_recv()
    wout_ref[...] = wall[...].reshape(BLOCK, HIDDEN)
    for copy in sends:
        copy.wait_send()


def dma(*shape):
    return pltpu.SemaphoreType.DMA(shape) if shape else pltpu.SemaphoreType.DMA


def shards(features, grad_out, weight, block_ids, block_vals, block_count, node_perm):
    rows, cols = lax.axis_size("row"), lax.axis_size("col")
    nz = rows // YL
    blk = (BLOCK, HIDDEN)
    ids = block_ids[0]
    piece = BLOCK // C // X

    source, vals = pl.pallas_call(
        gather_features,
        out_shape=(
            jax.ShapeDtypeStruct((rows,) + blk, BF16),
            jax.ShapeDtypeStruct(block_vals.shape[2:], BF16),
        ),
        in_specs=[VMEM, pl.BlockSpec(memory_space=pltpu.HBM)],
        out_specs=(VMEM, VMEM),
        scratch_shapes=[dma(nz), dma(nz), dma(nz), dma(nz), dma(), dma()],
        compiler_params=pltpu.CompilerParams(collective_id=0, has_side_effects=True, vmem_limit_bytes=WIDE),
        cost_estimate=LONG,
        name="gather_features",
    )(features, block_vals[0, 0])

    def multiply(src, targets, forward, name):
        return pl.pallas_call(
            lambda *refs: spmm(*refs, cols=rows, forward=forward),
            out_shape=jax.ShapeDtypeStruct((targets,) + blk, BF16),
            in_specs=[SMEM, SMEM, VMEM, VMEM],
            out_specs=VMEM,
            scratch_shapes=[
                pltpu.VMEM((targets + 1,) + blk, F32),
            ],
            compiler_params=pltpu.CompilerParams(vmem_limit_bytes=LIMIT),
            name=name,
        )(ids, block_count, vals, src)

    part = multiply(source, cols, True, "aggregate").reshape((C, X, YH) + blk)
    grads, wsum = pl.pallas_call(
        reduce_and_step,
        out_shape=(
            jax.ShapeDtypeStruct((C, X, YH) + blk, BF16),
            jax.ShapeDtypeStruct((piece, HIDDEN), F32),
        ),
        in_specs=[HBM, VMEM, VMEM],
        out_specs=(VMEM, VMEM),
        scratch_shapes=[
            pltpu.VMEM((X, YH) + blk, BF16),
            pltpu.VMEM((X, YH) + blk, BF16),
            pltpu.VMEM((X, YH) + blk, BF16),
            pltpu.VMEM((YH,) + blk, BF16),
            pltpu.VMEM((2, YH) + blk, BF16),
            pltpu.VMEM((YH,) + blk, BF16),
            pltpu.VMEM((YH,) + blk, BF16),
            pltpu.VMEM(blk, BF16),
            pltpu.VMEM((C, X, piece, HIDDEN), F32),
            pltpu.VMEM((C, X, piece, HIDDEN), F32),
            pltpu.VMEM((YL, YH, piece, HIDDEN), F32),
            dma(),
            dma(X), dma(X), dma(YH), dma(YH), dma(2, YH), dma(2, YH), dma(YH), dma(YH),
            dma(YH), dma(YH), dma(X, YH), dma(X, YH), dma(X, YH), dma(X, YH),
            dma(C, X), dma(C, X), dma(YL, YH), dma(YL, YH),
        ],
        compiler_params=pltpu.CompilerParams(collective_id=1, has_side_effects=True, vmem_limit_bytes=LIMIT),
        cost_estimate=LONG,
        name="reduce_and_step",
    )(part, grad_out, weight)
    back = multiply(grads.reshape((cols,) + blk), rows, False, "aggregate_back")
    scale = 1.0 / math.sqrt(rows * cols * BLOCK)
    return pl.pallas_call(
        lambda *refs: reduce_and_order(*refs, scale=scale),
        out_shape=(jax.ShapeDtypeStruct(blk, BF16), jax.ShapeDtypeStruct((BLOCK, HIDDEN), F32)),
        in_specs=[HBM, VMEM, VMEM],
        out_specs=(VMEM, VMEM),
        scratch_shapes=[
            pltpu.VMEM((nz,) + blk, BF16),
            pltpu.VMEM((nz,) + blk, BF16),
            pltpu.VMEM((nz,) + blk, BF16),
            pltpu.VMEM((nz,) + blk, BF16),
            pltpu.VMEM((nz, piece, HIDDEN), F32),
            pltpu.VMEM((C, X, piece, HIDDEN), F32),
            dma(),
            dma(nz), dma(nz), dma(nz), dma(nz), dma(nz), dma(nz), dma(C, X), dma(C, X),
        ],
        compiler_params=pltpu.CompilerParams(collective_id=2, has_side_effects=True, vmem_limit_bytes=LIMIT),
        cost_estimate=LONG,
        name="reduce_and_order",
    )(back.reshape((YL, nz) + blk), node_perm, wsum)


def solution(mesh):
    in_specs = (
        P(("col", "row"), None),
        P(("row", "col"), None),
        P(),
        P("row", "col", None),
        P("row", "col", None, None, None),
        P("row", "col"),
        P(("col", "row"), None),
    )
    out_specs = (P(("col", "row"), None), P())
    return jax.shard_map(shards, mesh=mesh, in_specs=in_specs, out_specs=out_specs, check_vma=False)
```

```python
import math

import jax
import jax.numpy as jnp
from jax import lax
from jax.experimental import pallas as pl
from jax.experimental.pallas import tpu as pltpu
from jax.sharding import PartitionSpec as P

BLOCK = 128
HIDDEN = 128
YL, C, X, YH = 2, 2, 4, 4
CHUNK = 8
LIMIT = 16 << 20
WIDE = 50_000_000
LONG = pl.CostEstimate(flops=0, bytes_accessed=50_000_000, transcendentals=0)
MESH = pl.DeviceIdType.MESH
F32, BF16 = jnp.float32, jnp.bfloat16
VMEM = pl.BlockSpec(memory_space=pltpu.VMEM)
SMEM = pl.BlockSpec(memory_space=pltpu.SMEM)
HBM = pl.BlockSpec(memory_space=pl.ANY)


def far_first(n):
    return sorted(range(1, n), key=lambda d: (-min(d, n - d), d))


def near_first(n):
    return sorted(range(1, n), key=lambda d: (min(d, n - d), d))


def remote(src, dst, send, recv, device):
    return pltpu.make_async_remote_copy(
        src_ref=src, dst_ref=dst, send_sem=send, recv_sem=recv, device_id=device, device_id_type=MESH
    )


def greet(devices):
    barrier = pltpu.get_barrier_semaphore()
    for device in devices:
        pl.semaphore_signal(barrier, inc=1, device_id=device, device_id_type=MESH)
    pl.semaphore_wait(barrier, len(devices))


def spread_along_z(z, nz, turn, at_z, slot, zs, zr, send):
    me = slot(z)
    for d in (2, nz - 2, 1, nz - 1):
        send(me, me, zs.at[d], zr.at[d], at_z(d))

    def arrive(d, sem):
        block = slot((z + nz - d) % nz)
        remote(block, block, zs.at[sem], zr.at[sem], at_z(d)).wait_recv()
        return block

    for d in (1, nz - 1):
        arrive(d, d)
        yield d
    for d in (2, nz - 2):
        block = arrive(d, d)
        onward = 1 if d == 2 else nz - 1
        send(block, block, zs.at[d + 1 if d == 2 else d - 1], zr.at[d + 1 if d == 2 else d - 1], at_z(onward))
        yield d
    back = slot((z + 2 * nz - 2 * turn) % nz)
    send(back, back, zs.at[4], zr.at[4], at_z(2 * nz + 2 * turn))
    for d in (3, nz - 3, 4):
        arrive(d, d)
        yield d


def gather_features(x_ref, vals_ref, out_ref, held_ref, zs, zr, ys, yr, loc, got):
    r, c = lax.axis_index("row"), lax.axis_index("col")
    nz = out_ref.shape[0] // YL
    z, y = r // YL, r % YL
    turn = 1 - 2 * (c % C)
    side = (z * YL + 1 - y, c)

    def at_z(d):
        return ((z + d) % nz * YL + y, c)

    own = pltpu.make_async_copy(x_ref, out_ref.at[r], loc)
    own.start()
    blocks = pltpu.make_async_copy(vals_ref, held_ref, got)
    blocks.start()
    greet([side] + [at_z(d) for d in (1, 2, nz - 2, nz - 1)])
    sends = []

    def send(*args):
        copy = remote(*args)
        copy.start()
        sends.append(copy)

    own.wait()
    send(out_ref.at[r], out_ref.at[r], ys.at[0], yr.at[0], side)
    for d in spread_along_z(z, nz, turn, at_z, lambda at: out_ref.at[at * YL + y], zs, zr, send):
        block = out_ref.at[(z + nz - d) % nz * YL + y]
        send(block, block, ys.at[d], yr.at[d], side)
    for d in range(nz):
        at = (z + nz - d) % nz * YL + 1 - y
        remote(x_ref, out_ref.at[at], ys.at[d], yr.at[d], side).wait_recv()
    for copy in sends:
        copy.wait_send()
    blocks.wait()


def multiply(ids_ref, count_ref, vals_ref, src_ref, out_ref, tab_ref, last_ref, acc, spot, head):
    count, cols, slots = count_ref[0, 0], src_ref.shape[0], ids_ref.shape[1]
    dead = acc.shape[0] - 1
    acc[...] = jnp.zeros_like(acc)
    for q in range(cols):
        spot[q] = 0

    def step(j, _):
        for half in range(0, CHUNK, 4):
            made = []
            for i in range(4):
                k = j * CHUNK + half + i
                p, q = ids_ref[0, k] // cols, ids_ref[0, k] % cols
                spot[q] = spot[q] + jnp.where(k < count, 1, 0)
                got = jnp.dot(vals_ref[k], src_ref[q], preferred_element_type=F32)
                made.append((jnp.where(k < count, p, dead), got))
            for to, got in made:
                acc[to] = acc[to] + got
        return 0

    lax.fori_loop(0, (count + CHUNK - 1) // CHUNK, step, 0)
    begin = jnp.int32(0)
    for q in range(cols):
        n = spot[q]
        spot[q] = begin
        head[q] = begin
        begin = begin + n
        last_ref[0, q] = jnp.where(n > 0, begin - 1, slots)

    def place(k, _):
        p, q = ids_ref[0, k] // cols, ids_ref[0, k] % cols
        at = spot[q]
        spot[q] = at + 1
        tab_ref[0, at] = k
        tab_ref[1, at] = p % C * (dead // C) + p // C
        tab_ref[2, at] = jnp.where(at == head[q], 0, 1)
        return 0

    def blank(k, _):
        for n in range(3):
            tab_ref[n, k] = 0
        return 0

    lax.fori_loop(0, count, place, 0)
    lax.fori_loop(count, slots, blank, 0)
    for b in range(dead):
        out_ref[b % C * (dead // C) + b // C] = acc[b].astype(BF16)


def reduce_step_and_back(
    part_ref, grad_ref, w_ref, tab_ref, last_ref, vals_ref, perm_ref, out_ref, wout_ref,
    part, sib, sx, rel, rx, sy, ry, share, wpart, wx, wy, grads, sums, back, zsib, sz, rz, wz, wall, loc,
    cs, cr, rs, rr, xs, xr, hs, hr, gys, gyr, gxs, gxr, gcs, gcr, wxs, wxr, wys, wyr,
    ys, yr, zs, zr, wzs, wzr, was, war,
    *, scale,
):
    r, c = lax.axis_index("row"), lax.axis_index("col")
    core = c % C
    x, h = c // C // YH, c // C % YH
    side = (r, (x * YH + h) * C + 1 - core)

    def at_x(d):
        return (r, ((x + d) % X * YH + h) * C + core)

    def at_h(d):
        return (r, (x * YH + (h + d) % YH) * C + core)

    z, y = r // YL, r % YL

    def at_xc(f, d):
        return (r, ((x + d) % X * YH + h) * C + (core + f) % C)

    def at_yh(f, d):
        return (z * YL + (y + f) % YL, (x * YH + (h + d) % YH) * C + core)

    across = [(f, d) for f in range(C) for d in range(X) if f or d]
    along = [(f, d) for f in range(YL) for d in range(YH) if f or d]
    mine = pltpu.make_async_copy(part_ref.at[core], part, loc)
    mine.start()
    nz = zsib.shape[0]
    side_y = at_yh(1, 0)

    def at_z(d):
        return ((z + d) % nz * YL + y, c)

    def shared(core, x, h):
        return grads.at[(core * X + x) * YH + h]

    greet(
        [at_xc(f, d) for f, d in across]
        + [at_yh(f, d) for f, d in along]
        + [at_z(d) for d in range(1, nz)]
    )
    sends = []

    def send(*args):
        copy = remote(*args)
        copy.start()
        sends.append(copy)

    def at(e):
        return (h + e) % YH

    for d in (2, 1, 3, 0):
        to = (x + d) % X
        send(part_ref.at[1 - core, to], sib.at[to], cs.at[d], cr.at[d], side)
    mine.wait()

    def have(d):
        to = (x + d) % X
        remote(part.at[to], sib.at[to], cs.at[d], cr.at[d], side).wait_recv()

    def pair(d, e):
        to = (x + d) % X
        return part[to, at(e)].astype(F32) + sib[to, at(e)].astype(F32)

    def push(d, e, total):
        to = (x + d) % X
        sx[to, at(e)] = total.astype(BF16)
        n = 0 if d == 1 else 1
        send(sx.at[to, at(e)], rx.at[n, at(e)], xs.at[n, e], xr.at[n, e], at_x(d))

    ahead = {2: 1, 0: 1, 1: X - 1, 3: X - 1}
    order = (2, 1, 3, 0)
    have(2)
    for e in order:
        sx[(x + 2) % X, at(e)] = pair(2, e).astype(BF16)
        send(sx.at[(x + 2) % X, at(e)], rel.at[at(e)], rs.at[e], rr.at[e], at_x(ahead[e]))
    for d in (1, X - 1):
        have(d)
        for e in order:
            if ahead[e] != d:
                push(d, e, pair(d, e))
    for e in order:
        remote(sx.at[x, at(e)], rel.at[at(e)], rs.at[e], rr.at[e], at_x(1)).wait_recv()
        push(ahead[e], e, pair(ahead[e], e) + rel[at(e)].astype(F32))
    have(0)

    def summed(e):
        for n in (0, 1):
            remote(share, rx.at[n, at(e)], xs.at[n, e], xr.at[n, e], at_x(1)).wait_recv()
        return pair(0, e) + (rx[0, at(e)].astype(F32) + rx[1, at(e)].astype(F32))

    for d in (2, 1, 3):
        to = at(d)
        sy[to] = summed(d).astype(BF16)
        send(sy.at[to], ry.at[h], hs.at[d], hr.at[d], at_h(d))
    aggregate = summed(0)
    for d in near_first(YH):
        frm = (h + YH - d) % YH
        remote(sy.at[frm], ry.at[frm], hs.at[d], hr.at[d], at_h(d)).wait_recv()
    for d in range(1, YH):
        aggregate = aggregate + ry[(h + d) % YH].astype(F32)
    agg_low = aggregate.astype(BF16)
    weight = w_ref[...]
    pre = jnp.dot(agg_low, weight, preferred_element_type=F32)
    sigma = 1.0 / (1.0 + jnp.exp(-pre))
    grad_pre = (grad_ref[...].astype(F32) * sigma * (1.0 + pre * (1.0 - sigma))).astype(BF16)
    flipped = lax.dot_general(weight, grad_pre, (((1,), (1,)), ((), ())), preferred_element_type=F32)
    share[...] = flipped.astype(BF16)
    for d in far_first(YH):
        send(share, shared(core, x, h), gys.at[d], gyr.at[d], at_h(d))
    for d in (1, X - 1):
        send(share, shared(core, x, h), gxs.at[d, 0], gxr.at[d, 0], at_x(d))
    send(share, shared(core, x, h), gcs.at[0, 0], gcr.at[0, 0], side)
    grads[(core * X + x) * YH + h] = flipped.astype(BF16)

    wpart[...] = lax.dot_general(
        agg_low, grad_pre, (((0,), (0,)), ((), ())), preferred_element_type=F32
    ).reshape(wpart.shape)
    for f, d in across:
        piece = wpart.at[(core + f) % C, (x + d) % X]
        send(piece, wx.at[core, x], wxs.at[f, d], wxr.at[f, d], at_xc(f, d))
    wx[core, x] = wpart[core, x]

    for d in near_first(YH):
        block = shared(core, x, (h + YH - d) % YH)
        remote(share, block, gys.at[d], gyr.at[d], at_h(d)).wait_recv()
        for e in (1, X - 1):
            send(block, block, gxs.at[e, d], gxr.at[e, d], at_x(e))
        send(block, block, gcs.at[0, d], gcr.at[0, d], side)

    for f, d in across:
        came = wx.at[(core + f) % C, (x + X - d) % X]
        remote(came, came, wxs.at[f, d], wxr.at[f, d], at_xc(f, d)).wait_recv()
    total = wx[0, 0]
    for n in range(1, C * X):
        total = total + wx[n // X, n % X]
    wy[y, h] = total
    for f, d in along:
        send(wy.at[y, h], wy.at[y, h], wys.at[f, d], wyr.at[f, d], at_yh(f, d))

    for e in (1, X - 1, 2):
        for d in [0] + near_first(YH):
            block = shared(core, (x + X - e) % X, (h + YH - d) % YH)
            remote(share, block, gxs.at[e, d], gxr.at[e, d], at_x(e)).wait_recv()
            if e == ahead[d]:
                send(block, block, gxs.at[2, d], gxr.at[2, d], at_x(e))
            send(block, block, gcs.at[e, d], gcr.at[e, d], side)

    for f, d in along:
        came = wy.at[(y + f) % YL, (h + YH - d) % YH]
        remote(came, came, wys.at[f, d], wyr.at[f, d], at_yh(f, d)).wait_recv()
    total = wy[0, 0]
    for n in range(1, YL * YH):
        total = total + wy[n // YH, n % YH]
    wz[z] = total
    for d in far_first(nz):
        send(wz.at[z], wz.at[z], wzs.at[d], wzr.at[d], at_z(d))

    for d in range(YH):
        for e in range(X):
            block = shared(1 - core, (x + X - e) % X, (h + YH - d) % YH)
            remote(share, block, gcs.at[e, d], gcr.at[e, d], side).wait_recv()

    sums[sums.shape[0] - 1] = jnp.zeros((BLOCK, HIDDEN), F32)

    def step(j, acc):
        for i in range(CHUNK):
            k = j * CHUNK + i
            got = jnp.dot(grads[tab_ref[1, k]], vals_ref[tab_ref[0, k]], preferred_element_type=F32)
            acc = acc * tab_ref[2, k].astype(F32) + got
            sums[k] = acc
        return acc

    lax.fori_loop(0, (sums.shape[0] - 1) // CHUNK, step, jnp.zeros((BLOCK, HIDDEN), F32))
    for d in far_first(nz) + [0]:
        to = (z + d) % nz
        back[to] = sums[last_ref[0, to * YL + 1 - y]].astype(BF16)
        send(back.at[to], zsib.at[to], ys.at[d], yr.at[d], side_y)

    def both(d):
        to = (z + d) % nz
        remote(back.at[to], zsib.at[to], ys.at[d], yr.at[d], side_y).wait_recv()
        return sums[last_ref[0, to * YL + y]] + zsib[to].astype(F32)

    for d in far_first(nz):
        to = (z + d) % nz
        sz[to] = both(d).astype(BF16)
        send(sz.at[to], rz.at[z], zs.at[d], zr.at[d], at_z(d))
    grad = both(0)

    for d in near_first(nz):
        came = wz.at[(z + nz - d) % nz]
        remote(came, came, wzs.at[d], wzr.at[d], at_z(d)).wait_recv()
    total = wz[0]
    for s in range(1, nz):
        total = total + wz[s]
    wall[core, x] = total * scale
    for f, d in across:
        send(wall.at[core, x], wall.at[core, x], was.at[f, d], war.at[f, d], at_xc(f, d))

    for d in near_first(nz):
        frm = (z + nz - d) % nz
        remote(sz.at[frm], rz.at[frm], zs.at[d], zr.at[d], at_z(d)).wait_recv()
        grad = grad + rz[frm].astype(F32)
    hot = lax.broadcasted_iota(jnp.int32, (BLOCK, BLOCK), 0) == perm_ref[...]
    hot = jnp.where(hot, 1.0, 0.0).astype(BF16)
    moved = jnp.dot(grad.astype(BF16), hot, preferred_element_type=F32)
    out_ref[...] = moved.T.astype(BF16)
    for f, d in across:
        came = wall.at[(core + f) % C, (x + X - d) % X]
        remote(came, came, was.at[f, d], war.at[f, d], at_xc(f, d)).wait_recv()
    wout_ref[...] = wall[...].reshape(BLOCK, HIDDEN)
    for copy in sends:
        copy.wait_send()


def dma(*shape):
    return pltpu.SemaphoreType.DMA(shape) if shape else pltpu.SemaphoreType.DMA


def shards(features, grad_out, weight, block_ids, block_vals, block_count, node_perm):
    rows, cols = lax.axis_size("row"), lax.axis_size("col")
    nz = rows // YL
    blk = (BLOCK, HIDDEN)
    ids = block_ids[0]
    piece = BLOCK // C // X

    source, vals = pl.pallas_call(
        gather_features,
        out_shape=(
            jax.ShapeDtypeStruct((rows,) + blk, BF16),
            jax.ShapeDtypeStruct(block_vals.shape[2:], BF16),
        ),
        in_specs=[VMEM, pl.BlockSpec(memory_space=pltpu.HBM)],
        out_specs=(VMEM, VMEM),
        scratch_shapes=[dma(nz), dma(nz), dma(nz), dma(nz), dma(), dma()],
        compiler_params=pltpu.CompilerParams(collective_id=0, has_side_effects=True, vmem_limit_bytes=WIDE),
        cost_estimate=LONG,
        name="gather_features",
    )(features, block_vals[0, 0])

    slots = block_ids.shape[-1]
    part, table, last = pl.pallas_call(
        multiply,
        out_shape=(
            jax.ShapeDtypeStruct((cols,) + blk, BF16),
            jax.ShapeDtypeStruct((3, slots), jnp.int32),
            jax.ShapeDtypeStruct((1, rows), jnp.int32),
        ),
        in_specs=[SMEM, SMEM, VMEM, VMEM],
        out_specs=(VMEM, SMEM, SMEM),
        scratch_shapes=[
            pltpu.VMEM((cols + 1,) + blk, F32),
            pltpu.SMEM((rows,), jnp.int32),
            pltpu.SMEM((rows,), jnp.int32),
        ],
        compiler_params=pltpu.CompilerParams(vmem_limit_bytes=LIMIT),
        name="aggregate",
    )(ids, block_count, vals, source)
    scale = 1.0 / math.sqrt(rows * cols * BLOCK)
    return pl.pallas_call(
        lambda *refs: reduce_step_and_back(*refs, scale=scale),
        out_shape=(jax.ShapeDtypeStruct(blk, BF16), jax.ShapeDtypeStruct((BLOCK, HIDDEN), F32)),
        in_specs=[HBM, VMEM, VMEM, SMEM, SMEM, VMEM, VMEM],
        out_specs=(VMEM, VMEM),
        scratch_shapes=[
            pltpu.VMEM((X, YH) + blk, BF16),
            pltpu.VMEM((X, YH) + blk, BF16),
            pltpu.VMEM((X, YH) + blk, BF16),
            pltpu.VMEM((YH,) + blk, BF16),
            pltpu.VMEM((2, YH) + blk, BF16),
            pltpu.VMEM((YH,) + blk, BF16),
            pltpu.VMEM((YH,) + blk, BF16),
            pltpu.VMEM(blk, BF16),
            pltpu.VMEM((C, X, piece, HIDDEN), F32),
            pltpu.VMEM((C, X, piece, HIDDEN), F32),
            pltpu.VMEM((YL, YH, piece, HIDDEN), F32),
            pltpu.VMEM((cols,) + blk, BF16),
            pltpu.VMEM((slots + 1,) + blk, F32),
            pltpu.VMEM((nz,) + blk, BF16),
            pltpu.VMEM((nz,) + blk, BF16),
            pltpu.VMEM((nz,) + blk, BF16),
            pltpu.VMEM((nz,) + blk, BF16),
            pltpu.VMEM((nz, piece, HIDDEN), F32),
            pltpu.VMEM((C, X, piece, HIDDEN), F32),
            dma(),
            dma(X), dma(X), dma(YH), dma(YH), dma(2, YH), dma(2, YH), dma(YH), dma(YH),
            dma(YH), dma(YH), dma(X, YH), dma(X, YH), dma(X, YH), dma(X, YH),
            dma(C, X), dma(C, X), dma(YL, YH), dma(YL, YH),
            dma(nz), dma(nz), dma(nz), dma(nz), dma(nz), dma(nz), dma(C, X), dma(C, X),
        ],
        compiler_params=pltpu.CompilerParams(
            collective_id=1, has_side_effects=True, vmem_limit_bytes=24 << 20
        ),
        cost_estimate=LONG,
        name="reduce_step_and_back",
    )(part.reshape((C, X, YH) + blk), grad_out, weight, table, last, vals, node_perm)


def solution(mesh):
    in_specs = (
        P(("col", "row"), None),
        P(("row", "col"), None),
        P(),
        P("row", "col", None),
        P("row", "col", None, None, None),
        P("row", "col"),
        P(("col", "row"), None),
    )
    out_specs = (P(("col", "row"), None), P())
    return jax.shard_map(shards, mesh=mesh, in_specs=in_specs, out_specs=out_specs, check_vma=False)
```

```python
import math

import jax
import jax.numpy as jnp
from jax import lax
from jax.experimental import pallas as pl
from jax.experimental.pallas import tpu as pltpu
from jax.sharding import PartitionSpec as P

BLOCK = 128
HIDDEN = 128
YL, C, X, YH = 2, 2, 4, 4
CHUNK = 8
LIMIT = 16 << 20
WIDE = 50_000_000
LONG = pl.CostEstimate(flops=0, bytes_accessed=50_000_000, transcendentals=0)
MESH = pl.DeviceIdType.MESH
F32, BF16 = jnp.float32, jnp.bfloat16
VMEM = pl.BlockSpec(memory_space=pltpu.VMEM)
SMEM = pl.BlockSpec(memory_space=pltpu.SMEM)
HBM = pl.BlockSpec(memory_space=pl.ANY)


def far_first(n):
    return sorted(range(1, n), key=lambda d: (-min(d, n - d), d))


def near_first(n):
    return sorted(range(1, n), key=lambda d: (min(d, n - d), d))


def remote(src, dst, send, recv, device):
    return pltpu.make_async_remote_copy(
        src_ref=src, dst_ref=dst, send_sem=send, recv_sem=recv, device_id=device, device_id_type=MESH
    )


def greet(devices):
    barrier = pltpu.get_barrier_semaphore()
    for device in devices:
        pl.semaphore_signal(barrier, inc=1, device_id=device, device_id_type=MESH)
    pl.semaphore_wait(barrier, len(devices))


def spread_along_z(z, nz, turn, at_z, slot, zs, zr, send):
    me = slot(z)
    for d in (2, nz - 2, 1, nz - 1):
        send(me, me, zs.at[d], zr.at[d], at_z(d))
    yield 0

    def arrive(d, sem):
        block = slot((z + nz - d) % nz)
        remote(block, block, zs.at[sem], zr.at[sem], at_z(d)).wait_recv()
        return block

    for d in (1, nz - 1):
        arrive(d, d)
        yield d
    for d in (2, nz - 2):
        block = arrive(d, d)
        onward = 1 if d == 2 else nz - 1
        send(block, block, zs.at[d + 1 if d == 2 else d - 1], zr.at[d + 1 if d == 2 else d - 1], at_z(onward))
        yield d
    back = slot((z + 2 * nz - 2 * turn) % nz)
    send(back, back, zs.at[4], zr.at[4], at_z(2 * nz + 2 * turn))
    for d in (3, nz - 3, 4):
        arrive(d, d)
        yield d


def order_slots(ids, count, cols, fast, groups):
    slots = ids.shape[1]
    down = lax.broadcasted_iota(jnp.int32, (slots, slots), 0)
    along = lax.broadcasted_iota(jnp.int32, (slots, slots), 1)
    ids = jnp.broadcast_to(ids.astype(F32), (slots, slots))
    flip = jnp.sum(jnp.where(down == along, ids, 0.0), axis=1, keepdims=True)
    p_down = jnp.floor(flip * (1.0 / cols))
    q_down = jnp.where(down < count, jnp.broadcast_to(flip - p_down * cols, (slots, slots)), 1.0 * cols)
    q_along = jnp.where(along < count, ids - jnp.floor(ids * (1.0 / cols)) * cols, 1.0 * cols)
    same = jnp.where((q_along == q_down) & (along < down), 1.0, 0.0)
    before = jnp.where(q_along < q_down, 1.0, 0.0) + same
    rank = jnp.sum(before, axis=1, keepdims=True)
    keep = jnp.minimum(jnp.sum(same, axis=1, keepdims=True), 1.0)
    half = jnp.floor(p_down * (1.0 / fast))
    source = (p_down - half * fast) * groups + half
    here = jnp.where(rank == along.astype(F32), 1.0, 0.0)

    def placed(value):
        return jnp.sum(here * value, axis=0, keepdims=True).astype(jnp.int32)

    column = along.astype(F32)
    upto = jnp.sum(jnp.where(q_down <= column, 1.0, 0.0), axis=0, keepdims=True)
    count_in = jnp.sum(jnp.where(q_down == column, 1.0, 0.0), axis=0, keepdims=True)
    last = jnp.where(count_in > 0.0, upto - 1.0, 1.0 * slots).astype(jnp.int32)
    return placed(down.astype(F32)), placed(source), placed(keep), last


def gather_features(x_ref, ids_ref, count_ref, vals_ref, out_ref, held_ref, tab_ref, zs, zr, ys, yr, loc, got, *, groups):
    r, c = lax.axis_index("row"), lax.axis_index("col")
    nz = out_ref.shape[0] // YL
    z, y = r // YL, r % YL
    turn = 1 - 2 * (c % C)
    side = (z * YL + 1 - y, c)

    def at_z(d):
        return ((z + d) % nz * YL + y, c)

    own = pltpu.make_async_copy(x_ref, out_ref.at[r], loc)
    own.start()
    blocks = pltpu.make_async_copy(vals_ref, held_ref, got)
    blocks.start()
    greet([side] + [at_z(d) for d in (1, 2, nz - 2, nz - 1)])
    sends = []

    def send(*args):
        copy = remote(*args)
        copy.start()
        sends.append(copy)

    own.wait()
    send(out_ref.at[r], out_ref.at[r], ys.at[0], yr.at[0], side)
    spread = spread_along_z(z, nz, turn, at_z, lambda at: out_ref.at[at * YL + y], zs, zr, send)
    next(spread)
    table = order_slots(ids_ref[...], count_ref[0, 0], nz * YL, C, groups)
    for n in range(4):
        tab_ref[n : n + 1, :] = table[n]
    for d in spread:
        block = out_ref.at[(z + nz - d) % nz * YL + y]
        send(block, block, ys.at[d], yr.at[d], side)
    for d in range(nz):
        at = (z + nz - d) % nz * YL + 1 - y
        remote(x_ref, out_ref.at[at], ys.at[d], yr.at[d], side).wait_recv()
    for copy in sends:
        copy.wait_send()
    blocks.wait()


def multiply(ids_ref, count_ref, vals_ref, src_ref, out_ref, acc):
    count, cols = count_ref[0, 0], src_ref.shape[0]
    dead = acc.shape[0] - 1
    acc[...] = jnp.zeros_like(acc)
    def step(j, _):
        for half in range(0, CHUNK, 4):
            made = []
            for i in range(4):
                k = j * CHUNK + half + i
                p, q = ids_ref[0, k] // cols, ids_ref[0, k] % cols
                got = jnp.dot(vals_ref[k], src_ref[q], preferred_element_type=F32)
                made.append((jnp.where(k < count, p, dead), got))
            for to, got in made:
                acc[to] = acc[to] + got
        return 0

    lax.fori_loop(0, (count + CHUNK - 1) // CHUNK, step, 0)
    for b in range(dead):
        out_ref[b % C * (dead // C) + b // C] = acc[b].astype(BF16)


def reduce_step_and_back(
    part_ref, grad_ref, w_ref, tab_ref, vals_ref, perm_ref, out_ref, wout_ref,
    part, sib, sx, rel, rx, sy, ry, share, wpart, wx, wy, grads, sums, back, zsib, sz, rz, wz, wall, loc,
    cs, cr, rs, rr, xs, xr, hs, hr, gys, gyr, gxs, gxr, gcs, gcr, wxs, wxr, wys, wyr,
    ys, yr, zs, zr, wzs, wzr, was, war,
    *, scale,
):
    r, c = lax.axis_index("row"), lax.axis_index("col")
    core = c % C
    x, h = c // C // YH, c // C % YH
    side = (r, (x * YH + h) * C + 1 - core)

    def at_x(d):
        return (r, ((x + d) % X * YH + h) * C + core)

    def at_h(d):
        return (r, (x * YH + (h + d) % YH) * C + core)

    z, y = r // YL, r % YL

    def at_xc(f, d):
        return (r, ((x + d) % X * YH + h) * C + (core + f) % C)

    def at_yh(f, d):
        return (z * YL + (y + f) % YL, (x * YH + (h + d) % YH) * C + core)

    across = [(f, d) for f in range(C) for d in range(X) if f or d]
    along = [(f, d) for f in range(YL) for d in range(YH) if f or d]
    mine = pltpu.make_async_copy(part_ref.at[core], part, loc)
    mine.start()
    nz = zsib.shape[0]
    side_y = at_yh(1, 0)

    def at_z(d):
        return ((z + d) % nz * YL + y, c)

    def shared(core, x, h):
        return grads.at[(core * X + x) * YH + h]

    greet(
        [at_xc(f, d) for f, d in across]
        + [at_yh(f, d) for f, d in along]
        + [at_z(d) for d in range(1, nz)]
    )
    sends = []

    def send(*args):
        copy = remote(*args)
        copy.start()
        sends.append(copy)

    def at(e):
        return (h + e) % YH

    for d in (2, 1, 3, 0):
        to = (x + d) % X
        send(part_ref.at[1 - core, to], sib.at[to], cs.at[d], cr.at[d], side)
    mine.wait()

    def have(d):
        to = (x + d) % X
        remote(part.at[to], sib.at[to], cs.at[d], cr.at[d], side).wait_recv()

    def pair(d, e):
        to = (x + d) % X
        return part[to, at(e)].astype(F32) + sib[to, at(e)].astype(F32)

    def push(d, e, total):
        to = (x + d) % X
        sx[to, at(e)] = total.astype(BF16)
        n = 0 if d == 1 else 1
        send(sx.at[to, at(e)], rx.at[n, at(e)], xs.at[n, e], xr.at[n, e], at_x(d))

    ahead = {2: 1, 0: 1, 1: X - 1, 3: X - 1}
    order = (2, 1, 3, 0)
    have(2)
    for e in order:
        sx[(x + 2) % X, at(e)] = pair(2, e).astype(BF16)
        send(sx.at[(x + 2) % X, at(e)], rel.at[at(e)], rs.at[e], rr.at[e], at_x(ahead[e]))
    for d in (1, X - 1):
        have(d)
        for e in order:
            if ahead[e] != d:
                push(d, e, pair(d, e))
    for e in order:
        remote(sx.at[x, at(e)], rel.at[at(e)], rs.at[e], rr.at[e], at_x(1)).wait_recv()
        push(ahead[e], e, pair(ahead[e], e) + rel[at(e)].astype(F32))
    have(0)

    def summed(e):
        for n in (0, 1):
            remote(share, rx.at[n, at(e)], xs.at[n, e], xr.at[n, e], at_x(1)).wait_recv()
        return pair(0, e) + (rx[0, at(e)].astype(F32) + rx[1, at(e)].astype(F32))

    for d in (2, 1, 3):
        to = at(d)
        sy[to] = summed(d).astype(BF16)
        send(sy.at[to], ry.at[h], hs.at[d], hr.at[d], at_h(d))
    aggregate = summed(0)
    for d in near_first(YH):
        frm = (h + YH - d) % YH
        remote(sy.at[frm], ry.at[frm], hs.at[d], hr.at[d], at_h(d)).wait_recv()
    for d in range(1, YH):
        aggregate = aggregate + ry[(h + d) % YH].astype(F32)
    agg_low = aggregate.astype(BF16)
    weight = w_ref[...]
    pre = jnp.dot(agg_low, weight, preferred_element_type=F32)
    sigma = 1.0 / (1.0 + jnp.exp(-pre))
    grad_pre = (grad_ref[...].astype(F32) * sigma * (1.0 + pre * (1.0 - sigma))).astype(BF16)
    flipped = lax.dot_general(weight, grad_pre, (((1,), (1,)), ((), ())), preferred_element_type=F32)
    share[...] = flipped.astype(BF16)
    for d in far_first(YH):
        send(share, shared(core, x, h), gys.at[d], gyr.at[d], at_h(d))
    for d in (1, X - 1):
        send(share, shared(core, x, h), gxs.at[d, 0], gxr.at[d, 0], at_x(d))
    send(share, shared(core, x, h), gcs.at[0, 0], gcr.at[0, 0], side)
    grads[(core * X + x) * YH + h] = flipped.astype(BF16)

    wpart[...] = lax.dot_general(
        agg_low, grad_pre, (((0,), (0,)), ((), ())), preferred_element_type=F32
    ).reshape(wpart.shape)
    for f, d in across:
        piece = wpart.at[(core + f) % C, (x + d) % X]
        send(piece, wx.at[core, x], wxs.at[f, d], wxr.at[f, d], at_xc(f, d))
    wx[core, x] = wpart[core, x]

    for d in near_first(YH):
        block = shared(core, x, (h + YH - d) % YH)
        remote(share, block, gys.at[d], gyr.at[d], at_h(d)).wait_recv()
        for e in (1, X - 1):
            send(block, block, gxs.at[e, d], gxr.at[e, d], at_x(e))
        send(block, block, gcs.at[0, d], gcr.at[0, d], side)

    for f, d in across:
        came = wx.at[(core + f) % C, (x + X - d) % X]
        remote(came, came, wxs.at[f, d], wxr.at[f, d], at_xc(f, d)).wait_recv()
    total = wx[0, 0]
    for n in range(1, C * X):
        total = total + wx[n // X, n % X]
    wy[y, h] = total
    for f, d in along:
        send(wy.at[y, h], wy.at[y, h], wys.at[f, d], wyr.at[f, d], at_yh(f, d))

    for e in (1, X - 1, 2):
        for d in [0] + near_first(YH):
            block = shared(core, (x + X - e) % X, (h + YH - d) % YH)
            remote(share, block, gxs.at[e, d], gxr.at[e, d], at_x(e)).wait_recv()
            if e == ahead[d]:
                send(block, block, gxs.at[2, d], gxr.at[2, d], at_x(e))
            send(block, block, gcs.at[e, d], gcr.at[e, d], side)

    for f, d in along:
        came = wy.at[(y + f) % YL, (h + YH - d) % YH]
        remote(came, came, wys.at[f, d], wyr.at[f, d], at_yh(f, d)).wait_recv()
    total = wy[0, 0]
    for n in range(1, YL * YH):
        total = total + wy[n // YH, n % YH]
    wz[z] = total
    for d in far_first(nz):
        send(wz.at[z], wz.at[z], wzs.at[d], wzr.at[d], at_z(d))

    for d in range(YH):
        for e in range(X):
            block = shared(1 - core, (x + X - e) % X, (h + YH - d) % YH)
            remote(share, block, gcs.at[e, d], gcr.at[e, d], side).wait_recv()

    sums[sums.shape[0] - 1] = jnp.zeros((BLOCK, HIDDEN), F32)

    def step(j, acc):
        for i in range(CHUNK):
            k = j * CHUNK + i
            got = jnp.dot(grads[tab_ref[1, k]], vals_ref[tab_ref[0, k]], preferred_element_type=F32)
            acc = acc * tab_ref[2, k].astype(F32) + got
            sums[k] = acc
        return acc

    lax.fori_loop(0, (sums.shape[0] - 1) // CHUNK, step, jnp.zeros((BLOCK, HIDDEN), F32))
    for d in far_first(nz) + [0]:
        to = (z + d) % nz
        back[to] = sums[tab_ref[3, to * YL + 1 - y]].astype(BF16)
        send(back.at[to], zsib.at[to], ys.at[d], yr.at[d], side_y)

    def both(d):
        to = (z + d) % nz
        remote(back.at[to], zsib.at[to], ys.at[d], yr.at[d], side_y).wait_recv()
        return sums[tab_ref[3, to * YL + y]] + zsib[to].astype(F32)

    for d in far_first(nz):
        to = (z + d) % nz
        sz[to] = both(d).astype(BF16)
        send(sz.at[to], rz.at[z], zs.at[d], zr.at[d], at_z(d))
    grad = both(0)

    for d in near_first(nz):
        came = wz.at[(z + nz - d) % nz]
        remote(came, came, wzs.at[d], wzr.at[d], at_z(d)).wait_recv()
    total = wz[0]
    for s in range(1, nz):
        total = total + wz[s]
    wall[core, x] = total * scale
    for f, d in across:
        send(wall.at[core, x], wall.at[core, x], was.at[f, d], war.at[f, d], at_xc(f, d))

    for d in near_first(nz):
        frm = (z + nz - d) % nz
        remote(sz.at[frm], rz.at[frm], zs.at[d], zr.at[d], at_z(d)).wait_recv()
        grad = grad + rz[frm].astype(F32)
    hot = lax.broadcasted_iota(jnp.int32, (BLOCK, BLOCK), 0) == perm_ref[...]
    hot = jnp.where(hot, 1.0, 0.0).astype(BF16)
    moved = jnp.dot(grad.astype(BF16), hot, preferred_element_type=F32)
    out_ref[...] = moved.T.astype(BF16)
    for f, d in across:
        came = wall.at[(core + f) % C, (x + X - d) % X]
        remote(came, came, was.at[f, d], war.at[f, d], at_xc(f, d)).wait_recv()
    wout_ref[...] = wall[...].reshape(BLOCK, HIDDEN)
    for copy in sends:
        copy.wait_send()


def dma(*shape):
    return pltpu.SemaphoreType.DMA(shape) if shape else pltpu.SemaphoreType.DMA


def shards(features, grad_out, weight, block_ids, block_vals, block_count, node_perm):
    rows, cols = lax.axis_size("row"), lax.axis_size("col")
    nz = rows // YL
    blk = (BLOCK, HIDDEN)
    ids = block_ids[0]
    piece = BLOCK // C // X

    slots = block_ids.shape[-1]
    source, vals, table = pl.pallas_call(
        lambda *refs: gather_features(*refs, groups=cols // C),
        out_shape=(
            jax.ShapeDtypeStruct((rows,) + blk, BF16),
            jax.ShapeDtypeStruct(block_vals.shape[2:], BF16),
            jax.ShapeDtypeStruct((4, slots), jnp.int32),
        ),
        in_specs=[VMEM, VMEM, SMEM, pl.BlockSpec(memory_space=pltpu.HBM)],
        out_specs=(VMEM, VMEM, VMEM),
        scratch_shapes=[dma(nz), dma(nz), dma(nz), dma(nz), dma(), dma()],
        compiler_params=pltpu.CompilerParams(collective_id=0, has_side_effects=True, vmem_limit_bytes=WIDE),
        cost_estimate=LONG,
        name="gather_features",
    )(features, ids, block_count, block_vals[0, 0])

    part = pl.pallas_call(
        multiply,
        out_shape=jax.ShapeDtypeStruct((cols,) + blk, BF16),
        in_specs=[SMEM, SMEM, VMEM, VMEM],
        out_specs=VMEM,
        scratch_shapes=[pltpu.VMEM((cols + 1,) + blk, F32)],
        compiler_params=pltpu.CompilerParams(vmem_limit_bytes=LIMIT),
        name="aggregate",
    )(ids, block_count, vals, source)
    scale = 1.0 / math.sqrt(rows * cols * BLOCK)
    return pl.pallas_call(
        lambda *refs: reduce_step_and_back(*refs, scale=scale),
        out_shape=(jax.ShapeDtypeStruct(blk, BF16), jax.ShapeDtypeStruct((BLOCK, HIDDEN), F32)),
        in_specs=[HBM, VMEM, VMEM, SMEM, VMEM, VMEM],
        out_specs=(VMEM, VMEM),
        scratch_shapes=[
            pltpu.VMEM((X, YH) + blk, BF16),
            pltpu.VMEM((X, YH) + blk, BF16),
            pltpu.VMEM((X, YH) + blk, BF16),
            pltpu.VMEM((YH,) + blk, BF16),
            pltpu.VMEM((2, YH) + blk, BF16),
            pltpu.VMEM((YH,) + blk, BF16),
            pltpu.VMEM((YH,) + blk, BF16),
            pltpu.VMEM(blk, BF16),
            pltpu.VMEM((C, X, piece, HIDDEN), F32),
            pltpu.VMEM((C, X, piece, HIDDEN), F32),
            pltpu.VMEM((YL, YH, piece, HIDDEN), F32),
            pltpu.VMEM((cols,) + blk, BF16),
            pltpu.VMEM((slots + 1,) + blk, F32),
            pltpu.VMEM((nz,) + blk, BF16),
            pltpu.VMEM((nz,) + blk, BF16),
            pltpu.VMEM((nz,) + blk, BF16),
            pltpu.VMEM((nz,) + blk, BF16),
            pltpu.VMEM((nz, piece, HIDDEN), F32),
            pltpu.VMEM((C, X, piece, HIDDEN), F32),
            dma(),
            dma(X), dma(X), dma(YH), dma(YH), dma(2, YH), dma(2, YH), dma(YH), dma(YH),
            dma(YH), dma(YH), dma(X, YH), dma(X, YH), dma(X, YH), dma(X, YH),
            dma(C, X), dma(C, X), dma(YL, YH), dma(YL, YH),
            dma(nz), dma(nz), dma(nz), dma(nz), dma(nz), dma(nz), dma(C, X), dma(C, X),
        ],
        compiler_params=pltpu.CompilerParams(
            collective_id=1, has_side_effects=True, vmem_limit_bytes=24 << 20
        ),
        cost_estimate=LONG,
        name="reduce_step_and_back",
    )(part.reshape((C, X, YH) + blk), grad_out, weight, table, vals, node_perm)


def solution(mesh):
    in_specs = (
        P(("col", "row"), None),
        P(("row", "col"), None),
        P(),
        P("row", "col", None),
        P("row", "col", None, None, None),
        P("row", "col"),
        P(("col", "row"), None),
    )
    out_specs = (P(("col", "row"), None), P())
    return jax.shard_map(shards, mesh=mesh, in_specs=in_specs, out_specs=out_specs, check_vma=False)
```
